128 devices in a mesh: scen: 8 (over y, x_lo), intr: 16 (over x_hi, z, core).
Axes of the slice: x: 4 (x_hi: 2, x_lo: 2; x = x_hi * 2 + x_lo), y: 4, z: 4, core: 2. Of those that a mesh axis runs over, the one named last changes fastest.
Arguments:
- inverse_panels: bfloat16 [32, 4096, 4096], P('scen', 'intr'), may hold values from -0.09375 to 0.09375
- border_columns: bfloat16 [32, 4096, 512], P('scen', 'intr'), may hold values from -6 to 6
- border_tiles: bfloat16 [32, 16, 4096, 128], P('scen', None, 'intr'), may hold values from -0.09375 to 0.09375
- tile_rows: int32 [32, 16], P('scen'), may hold values from 0 to 31
- tile_slabs: int32 [32, 16], P('scen'), may hold values from 0 to 1
- tile_count: int32 [32], P('scen'), may hold values from 1 to 16
- base_slab: float32 [4096, 512], P(('scen', 'intr')), may hold values from -6 to 6
- earlier_panels: bfloat16 [8, 4096, 128], P(None, ('scen', 'intr')), may hold values from -0.25 to 0.25
- used_panels: int32 [4], replicated, may hold values from 0 to 7, as said below
Outputs:
- schur_slab: float32 [4096, 512], P(('scen', 'intr'))
The draws below stay inside these ranges and needn't reach their ends.
Inputs may be any that keep to these rules, and one draw needn't show every extreme that they name: `used_panels`: distinct panel ids.
All inputs are finite; a program needn't handle non-finite values.
Results may differ from the reference program's by a relative error of at most 0.0026.
Values may be sent and summed in bfloat16 or wider, within the bound.
No kernel may reach another device: no remote copies, remote signals or barrier semaphores. Data moves between devices by JAX's collectives and lax.ppermute only.
A program may use at most 128 MiB of HBM per device.

```python
import jax
import jax.numpy as jnp
from jax import lax

SLAB_ROWS = 4096
COLS = 512
SLAB_W = 256
TILE = 128
LIST = 16
PANELS = 8
USED = 4
ROWS = 4096
SCEN = 32
NTILE = 32
NSLAB = 2


def draw_used_panels(key, part):
    return jax.random.permutation(key, PANELS)[:USED].astype(jnp.int32)


def with_ends(drawn, own_key, smallest, top_value):
    longest = drawn.shape.index(max(drawn.shape))
    spots = []
    for shift in (0, 1):
        where = [jax.random.randint(jax.random.fold_in(own_key, axis), (), 0, length) for axis, length in enumerate(drawn.shape)]
        where[longest] = (where[longest] + shift) % drawn.shape[longest]
        spots.append(tuple(where))
    return drawn.at[spots[0]].set(smallest).at[spots[1]].set(top_value)


def block_levels(own_key, shape, pieces, low, top_value):
    def one(axis_at, shards_of):
        draws = jax.random.uniform(jax.random.fold_in(jax.random.fold_in(own_key, 6), axis_at), (shards_of,), jnp.float32, low / len(pieces), top_value / len(pieces))
        return jnp.repeat(jnp.exp(draws), shape[axis_at] // shards_of).reshape((-1,) + (1,) * (len(shape) - axis_at - 1))

    gain = one(*pieces[0])
    for cut in pieces[1:]:
        gain = gain * one(*cut)
    return gain


def gaussian(own_key, shape, width, reach, shards=(), kind=jnp.bfloat16):
    drawn = jax.random.normal(own_key, shape, jnp.float32) * width
    if len(shards) > 0:
        drawn = block_levels(own_key, shape, shards, -0.22, 0.18) * drawn
    return jnp.clip(drawn, min=-reach, max=reach).astype(kind)


def setup_inputs(seed: int = 0) -> dict:
    key_list = jax.random.split(jax.random.key(seed), 10)
    inverse_panels = gaussian(key_list[0], (SCEN, ROWS, ROWS), ROWS ** -0.5, 0.09375, ((0, 8), (1, 16)))
    border_columns = gaussian(key_list[1], (SCEN, ROWS, COLS), 1.0, 6.0, ((0, 8), (1, 16)))
    border_tiles = gaussian(key_list[2], (SCEN, LIST, ROWS, TILE), ROWS ** -0.5, 0.09375, ((0, 8), (2, 16)))
    tile_rows = with_ends(jax.random.randint(key_list[3], (SCEN, LIST), 0, NTILE), jax.random.fold_in(key_list[3], 1), 0, NTILE - 1).astype(jnp.int32)
    tile_slabs = with_ends(jax.random.randint(key_list[4], (SCEN, LIST), 0, NSLAB), jax.random.fold_in(key_list[4], 1), 0, NSLAB - 1).astype(jnp.int32)
    tile_count = with_ends(jax.random.randint(key_list[5], (SCEN,), 1, LIST + 1), jax.random.fold_in(key_list[5], 1), 1, LIST).astype(jnp.int32)
    base_slab = gaussian(key_list[6], (SLAB_ROWS, COLS), 1.0, 6.0, ((0, 128),), jnp.float32)
    earlier_panels = gaussian(key_list[7], (PANELS, SLAB_ROWS, TILE), (USED * TILE) ** -0.5, 0.25, ((1, 128),))
    used_panels = draw_used_panels(jax.random.fold_in(key_list[9], 71), 0)
    return dict(inverse_panels=inverse_panels, border_columns=border_columns, border_tiles=border_tiles, tile_rows=tile_rows, tile_slabs=tile_slabs, tile_count=tile_count, base_slab=base_slab, earlier_panels=earlier_panels, used_panels=used_panels)


def reference(inverse_panels, border_columns, border_tiles, tile_rows, tile_slabs, tile_count, base_slab, earlier_panels, used_panels):
    nslab = COLS // SLAB_W
    targets = jnp.arange(NTILE * nslab, dtype=jnp.int32)
    positions = jnp.arange(LIST, dtype=jnp.int32)

    def one_scenario(total, items):
        inverse, columns, tiles, rows, slabs, count = items
        applied = jnp.dot(inverse, columns, preferred_element_type=jnp.float32).astype(jnp.bfloat16)
        split = applied.reshape(ROWS, nslab, SLAB_W)
        chosen = jnp.transpose(split[:, slabs, :], (1, 0, 2))
        product = jnp.einsum('lrt,lrw->ltw', tiles.astype(jnp.float32), chosen.astype(jnp.float32))
        live = (positions < count).astype(jnp.float32)
        places = (rows * nslab + slabs).astype(jnp.int32)
        onehot = (places[:, None] == targets[None, :]).astype(jnp.float32) * live[:, None]
        block = jnp.dot(onehot.T, product.reshape(LIST, TILE * SLAB_W), precision=lax.Precision.HIGHEST)
        return total + block, None

    start = jnp.zeros((NTILE * nslab, TILE * SLAB_W), jnp.float32)
    total, unused = lax.scan(one_scenario, start, (inverse_panels, border_columns, border_tiles, tile_rows, tile_slabs, tile_count))
    coupling = total.reshape(NTILE, nslab, TILE, SLAB_W).transpose(0, 2, 1, 3).reshape(SLAB_ROWS, COLS)
    chosen_panels = earlier_panels[used_panels].astype(jnp.float32)
    earlier = jnp.einsum('prt,pct->rc', chosen_panels, chosen_panels[:, :COLS, :])
    return base_slab - coupling - earlier
```

```python
import functools

import jax
import jax.numpy as jnp
from jax import lax
from jax.experimental import pallas as pl
from jax.experimental.pallas import tpu as pltpu
from jax.sharding import PartitionSpec as P

COLS = 512
SLAB_W = 256
TILE = 128
LIST = 16
NTILE = 32
HERE = 4
ROWS_HERE = 256
AXES = ("y", "xl", "xh", "z", "c")
CHIPS = ("y", "xl", "xh", "z")


def device_at(x, y, z, c):
    return (((y * 2 + x % 2) * 2 + x // 2) * 4 + z) * 2 + c


def everyone():
    return [(x, y, z, c) for x in range(4) for y in range(4) for z in range(4) for c in range(2)]


def moved(array, dx=0, dy=0, dz=0, dc=0):
    pairs = [
        (device_at(x, y, z, c), device_at((x + dx) % 4, (y + dy) % 4, (z + dz) % 4, (c + dc) % 2))
        for x, y, z, c in everyone()
    ]
    return lax.ppermute(array, AXES, sorted(pairs))


def sent(array, goes):
    pairs = []
    for x, y, z, c in everyone():
        for target in goes(x, y, z, c):
            pairs.append((device_at(x, y, z, c), device_at(*target)))
    return lax.ppermute(array, AXES, sorted(pairs))


def apply_body(place, inv_own, inv_par, *rest):
    blocks, out = rest[:8], rest[8]
    xh, z, c = place[0], place[1], place[2]
    own = jnp.zeros((ROWS_HERE, SLAB_W), jnp.float32)
    par = jnp.zeros((ROWS_HERE, SLAB_W), jnp.float32)
    for far in range(2):
        for step, shift in enumerate((0, 3, 1, 2)):
            chip = lax.rem(xh + far, 2) * 4 + lax.rem(z + shift, 4)
            block = blocks[far * 4 + step]
            for half in range(2):
                core = c if half == 0 else 1 - c
                at = pl.multiple_of((chip * 2 + core) * ROWS_HERE, ROWS_HERE)
                piece = block[0, half * ROWS_HERE : (half + 1) * ROWS_HERE, :]
                own += jnp.dot(
                    inv_own[0, :, pl.ds(at, ROWS_HERE)], piece, preferred_element_type=jnp.float32
                )
                par += jnp.dot(
                    inv_par[0, :, pl.ds(at, ROWS_HERE)], piece, preferred_element_type=jnp.float32
                )
    out[0, :ROWS_HERE, :] = own.astype(jnp.bfloat16)
    out[0, ROWS_HERE:, :] = par.astype(jnp.bfloat16)


def apply_group(place, inv_own, inv_par, first, blocks):
    inv_spec = pl.BlockSpec((1, ROWS_HERE, 4096), lambda g, p: (g + first, 0, 0))
    specs = [
        pl.BlockSpec((1, 2 * ROWS_HERE, SLAB_W), functools.partial(lambda o, g, p: (g + o, 0, 0), offset))
        for _, offset in blocks
    ]
    return pl.pallas_call(
        apply_body,
        out_shape=jax.ShapeDtypeStruct((2, 2 * ROWS_HERE, SLAB_W), jnp.bfloat16),
        grid_spec=pltpu.PrefetchScalarGridSpec(
            num_scalar_prefetch=1,
            grid=(2,),
            in_specs=[inv_spec, inv_spec] + specs,
            out_specs=pl.BlockSpec((1, 2 * ROWS_HERE, SLAB_W), lambda g, p: (g, 0, 0)),
        ),
        cost_estimate=pl.CostEstimate(
            flops=2 * 2 * 512 * 4096 * 256, bytes_accessed=12 << 20, transcendentals=0
        ),
        name="apply_group",
    )(place, inv_own, inv_par, *[array for array, _ in blocks])


def couple_body(rows, slabs, counts, place, t_own, t_par, first, second, out, acc):
    s = pl.program_id(0)
    c = place[2]

    @pl.when(s == 0)
    def _():
        acc[...] = jnp.zeros_like(acc)

    def run(applied, g):
        def step(l, carry):
            @pl.when(slabs[s, l] == c)
            def _():
                row = rows[s, l]
                term = lax.dot_general(
                    t_own[0, l],
                    applied[g, :ROWS_HERE, :],
                    (((0,), (0,)), ((), ())),
                    preferred_element_type=jnp.float32,
                )
                term += lax.dot_general(
                    t_par[0, l],
                    applied[g, ROWS_HERE:, :],
                    (((0,), (0,)), ((), ())),
                    preferred_element_type=jnp.float32,
                )
                acc[row] += term

            return carry

        lax.fori_loop(0, counts[s], step, 0)

    @pl.when(s < 2)
    def _():
        run(first, s)

    @pl.when(s >= 2)
    def _():
        run(second, s - 2)

    @pl.when(s == HERE - 1)
    def _():
        out[...] = acc[...].astype(jnp.bfloat16)


def couple(rows, slabs, counts, place, t_own, t_par, first, second):
    tile_spec = pl.BlockSpec((1, LIST, ROWS_HERE, TILE), lambda s, *_: (s, 0, 0, 0))
    whole = pl.BlockSpec((2, 2 * ROWS_HERE, SLAB_W), lambda s, *_: (0, 0, 0))
    return pl.pallas_call(
        couple_body,
        out_shape=jax.ShapeDtypeStruct((NTILE, TILE, SLAB_W), jnp.bfloat16),
        grid_spec=pltpu.PrefetchScalarGridSpec(
            num_scalar_prefetch=4,
            grid=(HERE,),
            in_specs=[tile_spec, tile_spec, whole, whole],
            out_specs=pl.BlockSpec((NTILE, TILE, SLAB_W), lambda s, *_: (0, 0, 0)),
            scratch_shapes=[pltpu.VMEM((NTILE, TILE, SLAB_W), jnp.float32)],
        ),
        cost_estimate=pl.CostEstimate(
            flops=64 * 2 * 128 * 512 * 256, bytes_accessed=12 << 20, transcendentals=0
        ),
        name="couple",
    )(rows, slabs, counts, place, t_own, t_par, first, second)


def earlier_term(earlier_panels, used_panels, place):
    y = lax.axis_index("y")
    xl = lax.axis_index("xl")
    xh, z, c = place
    chosen = earlier_panels[used_panels]
    got = sent(chosen, lambda x, y, z, c: [(x, 1, z, c)] if y == 0 and x % 2 == 0 else [])
    top = jnp.where(y == 1, got, chosen)
    got = sent(top, lambda x, y, z, c: [(x, 3 - y, z, c)] if y < 2 and x % 2 == 0 else [])
    top = jnp.where(y >= 2, got, top)
    got = sent(top, lambda x, y, z, c: [(x + 1, y, z, c)] if x % 2 == 0 else [])
    top = jnp.where(xl == 1, got, top)
    other = moved(top, dc=1)
    pair = jnp.stack([jnp.where(c == 0, top, other), jnp.where(c == 0, other, top)])
    line = jnp.stack([pair, moved(pair, dz=-1), moved(pair, dz=2), moved(pair, dz=1)])
    far = moved(line, dx=2)
    plane = jnp.stack([line, far])
    at_x = lax.rem(jnp.arange(2, dtype=jnp.int32) + xh, 2)
    at_z = lax.rem(jnp.arange(4, dtype=jnp.int32) + 4 - z, 4)
    order = (at_x[:, None] * 4 + at_z[None, :]).reshape(8)
    ordered = plane.reshape(8, 2, 4, 32, TILE)[order]
    top_rows = ordered.reshape(16, 4, 32, TILE).transpose(1, 0, 2, 3).reshape(4, COLS, TILE)
    return jnp.einsum("prt,pct->rc", chosen, top_rows, preferred_element_type=jnp.float32)


def on_device(
    inverse_panels,
    border_columns,
    border_tiles,
    tile_rows,
    tile_slabs,
    tile_count,
    base_slab,
    earlier_panels,
    used_panels,
):
    xh = lax.axis_index("xh")
    z = lax.axis_index("z")
    c = lax.axis_index("c")
    place = jnp.stack([xh, z, c]).astype(jnp.int32)

    keep = lax.dynamic_slice_in_dim(border_columns, c * SLAB_W, SLAB_W, 2)
    give = lax.dynamic_slice_in_dim(border_columns, (1 - c) * SLAB_W, SLAB_W, 2)
    mine = jnp.concatenate([keep, moved(give, dc=1)], axis=1)
    inv_par = moved(inverse_panels, dc=1)
    t_par = moved(border_tiles, dc=1)

    a0, b0 = mine[:2], mine[2:]
    bx = moved(b0, dx=2)
    am = moved(a0, dz=1)
    ap = moved(a0, dz=-1)
    xa0 = moved(a0, dx=2)
    a2 = jnp.concatenate([moved(am[:1], dz=1), moved(ap[1:], dz=-1)], axis=0)
    bb = jnp.concatenate([b0, bx], axis=0)
    bm = moved(bb, dz=1)
    bp = moved(bb, dz=-1)
    xa1 = moved(jnp.concatenate([am, ap], axis=0), dx=2)
    b2 = moved(bm[:2], dz=1)
    xb2 = moved(bp[2:], dz=-1)
    xa2 = moved(a2, dx=2)

    first = apply_group(
        place,
        inverse_panels,
        inv_par,
        0,
        [(a0, 0), (am, 0), (ap, 0), (a2, 0), (xa0, 0), (xa1, 0), (xa1, 2), (xa2, 0)],
    )
    second = apply_group(
        place,
        inverse_panels,
        inv_par,
        2,
        [(bb, 0), (bm, 0), (bp, 0), (b2, 0), (bb, 2), (bm, 2), (bp, 2), (xb2, 0)],
    )
    part = couple(tile_rows, tile_slabs, tile_count, place, border_tiles, t_par, first, second)
    spread = lax.all_to_all(part.reshape(4096, SLAB_W), CHIPS, 0, 0, tiled=True)
    total = spread.reshape(64, 2, 32, SLAB_W).astype(jnp.float32).sum(axis=0)
    held = jnp.where(c == 0, total[0], total[1])
    got = moved(jnp.where(c == 0, total[1], total[0]), dc=1)
    coupling = jnp.concatenate(
        [jnp.where(c == 0, held, got), jnp.where(c == 0, got, held)], axis=1
    )
    earlier = earlier_term(earlier_panels, used_panels, (xh, z, c))
    return base_slab - coupling - earlier


def solution(mesh):
    split = jax.sharding.Mesh(mesh.devices.reshape(4, 2, 2, 4, 2), AXES)
    scen, intr = ("y", "xl"), ("xh", "z", "c")
    return jax.shard_map(
        on_device,
        mesh=split,
        in_specs=(
            P(scen, intr, None),
            P(scen, intr, None),
            P(scen, None, intr, None),
            P(scen, None),
            P(scen, None),
            P(scen),
            P(AXES, None),
            P(None, AXES, None),
            P(),
        ),
        out_specs=P(AXES, None),
        check_vma=False,
    )
```

```python
import functools

import jax
import jax.numpy as jnp
from jax import lax
from jax.experimental import pallas as pl
from jax.experimental.pallas import tpu as pltpu
from jax.sharding import PartitionSpec as P


COLS = 512
SLAB_W = 256
TILE = 128
LIST = 16
NTILE = 32
HERE = 4
ROWS_HERE = 256
CHIP_ROWS = 512
BATCH = 4
AXES = ("y", "xl", "xh", "z", "c")
CHIPS = ("y", "xl", "xh", "z")


def device_at(x, y, z, c):
    return (((y * 2 + x % 2) * 2 + x // 2) * 4 + z) * 2 + c


def everyone():
    return [(x, y, z, c) for x in range(4) for y in range(4) for z in range(4) for c in range(2)]


def moved(array, dx=0, dy=0, dz=0, dc=0):
    pairs = [
        (device_at(x, y, z, c), device_at((x + dx) % 4, (y + dy) % 4, (z + dz) % 4, (c + dc) % 2))
        for x, y, z, c in everyone()
    ]
    return lax.ppermute(array, AXES, sorted(pairs))


def sent(array, goes):
    pairs = []
    for x, y, z, c in everyone():
        for target in goes(x, y, z, c):
            pairs.append((device_at(x, y, z, c), device_at(*target)))
    return lax.ppermute(array, AXES, sorted(pairs))


def chip_of(place, where):
    far, shift = where
    return lax.rem(place[0] + far, 2) * 4 + lax.rem(place[1] + shift, 4)


def stage_specs(group_a, group_b):
    slots = max(len(group_a), len(group_b))
    block_specs = [
        pl.BlockSpec(
            (1, CHIP_ROWS, SLAB_W),
            functools.partial(lambda o, s, p, *_: (jnp.minimum(s, 1) + o, 0, 0), offset),
        )
        for _, offset, _ in group_a
    ] + [
        pl.BlockSpec(
            (1, CHIP_ROWS, SLAB_W),
            functools.partial(lambda o, s, p, *_: (jnp.maximum(s - 2, 0) + o, 0, 0), offset),
        )
        for _, offset, _ in group_b
    ]

    def columns(i, s, p, *_):
        at_a = chip_of(p, group_a[min(i, len(group_a) - 1)][2])
        at_b = chip_of(p, group_b[min(i, len(group_b) - 1)][2])
        return (s, 0, jnp.where(s < 2, at_a, at_b))

    inverse_specs = [
        pl.BlockSpec((1, ROWS_HERE, CHIP_ROWS), functools.partial(columns, i)) for i in range(slots)
    ]
    return block_specs, inverse_specs


def added(inv_own, inv_par, blocks):
    total = None
    for own, par, block in zip(inv_own, inv_par, blocks):
        left = jnp.concatenate([own[0], par[0]], axis=0)
        term = jnp.dot(left, block[0], preferred_element_type=jnp.float32)
        total = term if total is None else total + term
    return total


def stage_body(count_a, count_b, has_sum, place, *refs):
    s = pl.program_id(0)
    slots = max(count_a, count_b)
    blocks = refs[: count_a + count_b]
    own = refs[count_a + count_b : count_a + count_b + slots]
    par = refs[count_a + count_b + slots : count_a + count_b + 2 * slots]
    out = refs[-1]
    for here, group, count in ((s < 2, blocks[:count_a], count_a), (s >= 2, blocks[count_a:], count_b)):

        @pl.when(here)
        def _():
            total = added(own[:count], par[:count], group)
            if has_sum:
                total = total + refs[-2][0]
            out[0] = total


def stage(place, inv_own, inv_par, group_a, group_b, so_far=None):
    block_specs, inverse_specs = stage_specs(group_a, group_b)
    sum_spec = pl.BlockSpec((1, CHIP_ROWS, SLAB_W), lambda s, p: (s, 0, 0))
    slots = len(inverse_specs)
    units = 2 * (len(group_a) + len(group_b))
    return pl.pallas_call(
        functools.partial(stage_body, len(group_a), len(group_b), so_far is not None),
        out_shape=jax.ShapeDtypeStruct((HERE, CHIP_ROWS, SLAB_W), jnp.float32),
        grid_spec=pltpu.PrefetchScalarGridSpec(
            num_scalar_prefetch=1,
            grid=(HERE,),
            in_specs=block_specs
            + inverse_specs * 2
            + ([] if so_far is None else [sum_spec]),
            out_specs=sum_spec,
        ),
        cost_estimate=pl.CostEstimate(
            flops=units * 2 * 512 * 512 * 256, bytes_accessed=units << 19, transcendentals=0
        ),
    )(
        place,
        *[array for array, _, _ in group_a + group_b],
        *([inv_own] * slots),
        *([inv_par] * slots),
        *([] if so_far is None else [so_far]),
    )


def prepare_body(slabs, counts, place, t_own, t_par, out):
    s = pl.program_id(0)

    def step(l, found):
        hit = slabs[s, l] == place[2]

        @pl.when(hit)
        def _():
            out[0, found, :, :ROWS_HERE] = t_own[0, l].T
            out[0, found, :, ROWS_HERE:] = t_par[0, l].T

        return found + hit.astype(jnp.int32)

    lax.fori_loop(0, counts[s], step, jnp.int32(0))


def prepare(slabs, counts, place, t_own, t_par):
    tile_spec = pl.BlockSpec((1, LIST, ROWS_HERE, TILE), lambda s, *_: (s, 0, 0, 0))
    return pl.pallas_call(
        prepare_body,
        out_shape=jax.ShapeDtypeStruct((HERE, LIST, TILE, CHIP_ROWS), jnp.bfloat16),
        grid_spec=pltpu.PrefetchScalarGridSpec(
            num_scalar_prefetch=3,
            grid=(HERE,),
            in_specs=[tile_spec, tile_spec],
            out_specs=pl.BlockSpec((1, LIST, TILE, CHIP_ROWS), lambda s, *_: (s, 0, 0, 0)),
        ),
        cost_estimate=pl.CostEstimate(flops=1 << 20, bytes_accessed=16 << 20, transcendentals=0),
        name="prepare",
    )(slabs, counts, place, t_own, t_par)


def couple_body(count_a, count_b, place, rows, slabs, counts, *refs):
    s = pl.program_id(0)
    slots = max(count_a, count_b)
    blocks = refs[: count_a + count_b]
    own = refs[count_a + count_b : count_a + count_b + slots]
    par = refs[count_a + count_b + slots : count_a + count_b + 2 * slots]
    so_far, tiles, out, acc, applied, found_rows = refs[-6:]

    @pl.when(s == 0)
    def _():
        acc[...] = jnp.zeros_like(acc)

    for here, group, count in ((s < 2, blocks[:count_a], count_a), (s >= 2, blocks[count_a:], count_b)):

        @pl.when(here)
        def _():
            total = added(own[:count], par[:count], group) + so_far[0]
            applied[...] = total.astype(jnp.bfloat16)

    def look(l, found):
        hit = slabs[s, l] == place[2]

        @pl.when(hit)
        def _():
            found_rows[found] = rows[s, l]

        return found + hit.astype(jnp.int32)

    found = lax.fori_loop(0, counts[s], look, jnp.int32(0))

    def step(b, carry):
        left = tiles[0, pl.ds(b * BATCH, BATCH)].reshape(BATCH * TILE, CHIP_ROWS)
        term = jnp.dot(left, applied[...], preferred_element_type=jnp.float32)
        for j in range(BATCH):

            @pl.when(b * BATCH + j < found)
            def _():
                acc[found_rows[b * BATCH + j]] += term[j * TILE : (j + 1) * TILE]

        return carry

    lax.fori_loop(0, (found + BATCH - 1) // BATCH, step, 0)

    @pl.when(s == HERE - 1)
    def _():
        out[...] = acc[...].astype(jnp.bfloat16)


def couple(place, rows, slabs, counts, inv_own, inv_par, group_a, group_b, so_far, tiles):
    block_specs, inverse_specs = stage_specs(group_a, group_b)
    slots = len(inverse_specs)
    return pl.pallas_call(
        functools.partial(couple_body, len(group_a), len(group_b)),
        out_shape=jax.ShapeDtypeStruct((NTILE, TILE, SLAB_W), jnp.bfloat16),
        grid_spec=pltpu.PrefetchScalarGridSpec(
            num_scalar_prefetch=4,
            grid=(HERE,),
            in_specs=block_specs
            + inverse_specs * 2
            + [
                pl.BlockSpec((1, CHIP_ROWS, SLAB_W), lambda s, *_: (s, 0, 0)),
                pl.BlockSpec((1, LIST, TILE, CHIP_ROWS), lambda s, *_: (s, 0, 0, 0)),
            ],
            out_specs=pl.BlockSpec((NTILE, TILE, SLAB_W), lambda s, *_: (0, 0, 0)),
            scratch_shapes=[
                pltpu.VMEM((NTILE, TILE, SLAB_W), jnp.float32),
                pltpu.VMEM((CHIP_ROWS, SLAB_W), jnp.bfloat16),
                pltpu.SMEM((LIST,), jnp.int32),
            ],
        ),
        cost_estimate=pl.CostEstimate(flops=3 << 30, bytes_accessed=16 << 20, transcendentals=0),
        name="couple",
    )(
        place,
        rows,
        slabs,
        counts,
        *[array for array, _, _ in group_a + group_b],
        *([inv_own] * slots),
        *([inv_par] * slots),
        so_far,
        tiles,
    )


def earlier_term(earlier_panels, used_panels, where):
    y = lax.axis_index("y")
    xl = lax.axis_index("xl")
    xh, z, c = where
    chosen = earlier_panels[used_panels]
    got = sent(chosen, lambda x, y, z, c: [(x, 1, z, c)] if y == 0 and x % 2 == 0 else [])
    top = jnp.where(y == 1, got, chosen)
    got = sent(top, lambda x, y, z, c: [(x, 3 - y, z, c)] if y < 2 and x % 2 == 0 else [])
    top = jnp.where(y >= 2, got, top)
    got = sent(top, lambda x, y, z, c: [(x + 1, y, z, c)] if x % 2 == 0 else [])
    top = jnp.where(xl == 1, got, top)
    other = moved(top, dc=1)
    pair = jnp.stack([jnp.where(c == 0, top, other), jnp.where(c == 0, other, top)])
    line = jnp.stack([pair, moved(pair, dz=-1), moved(pair, dz=2), moved(pair, dz=1)])
    far = moved(line, dx=2)
    plane = jnp.stack([line, far])
    at_x = lax.rem(jnp.arange(2, dtype=jnp.int32) + xh, 2)
    at_z = lax.rem(jnp.arange(4, dtype=jnp.int32) + 4 - z, 4)
    order = (at_x[:, None] * 4 + at_z[None, :]).reshape(8)
    ordered = plane.reshape(8, 2, 4, 32, TILE)[order]
    top_rows = ordered.reshape(16, 4, 32, TILE).transpose(1, 0, 2, 3).reshape(4, COLS, TILE)
    return jnp.einsum("prt,pct->rc", chosen, top_rows, preferred_element_type=jnp.float32)


def on_device(
    inverse_panels,
    border_columns,
    border_tiles,
    tile_rows,
    tile_slabs,
    tile_count,
    base_slab,
    earlier_panels,
    used_panels,
):
    xh = lax.axis_index("xh")
    z = lax.axis_index("z")
    c = lax.axis_index("c")
    place = jnp.stack([xh, z, c]).astype(jnp.int32)

    keep = lax.dynamic_slice_in_dim(border_columns, c * SLAB_W, SLAB_W, 2)
    give = lax.dynamic_slice_in_dim(border_columns, (1 - c) * SLAB_W, SLAB_W, 2)
    got = moved(give, dc=1)
    mine = jnp.concatenate([jnp.where(c == 0, keep, got), jnp.where(c == 0, got, keep)], axis=1)
    inv_par = moved(inverse_panels, dc=1)
    t_par = moved(border_tiles, dc=1)

    a0, b0 = mine[:2], mine[2:]
    bx = moved(b0, dx=2)
    am = moved(a0, dz=1)
    ap = moved(a0, dz=-1)
    xa0 = moved(a0, dx=2)
    bb = jnp.concatenate([b0, bx], axis=0)
    bm = moved(bb, dz=1)
    bp = moved(bb, dz=-1)
    xa1 = moved(jnp.concatenate([am, ap], axis=0), dx=2)
    a2m = moved(am[:1], dz=1)
    a2p = moved(ap[1:], dz=-1)
    a2 = jnp.concatenate([a2m, a2p], axis=0)
    xa2 = moved(a2, dx=2)
    b2 = moved(bm[:2], dz=1)
    xb2 = moved(bp[2:], dz=-1)

    tiles = prepare(tile_slabs, tile_count, place, border_tiles, t_par)
    so_far = stage(
        place,
        inverse_panels,
        inv_par,
        [(a0, 0, (0, 0)), (am, 0, (0, 3)), (ap, 0, (0, 1)), (xa0, 0, (1, 0))],
        [(bb, 0, (0, 0)), (bb, 2, (1, 0))],
    )
    so_far = stage(
        place,
        inverse_panels,
        inv_par,
        [(a2, 0, (0, 2)), (xa1, 0, (1, 3)), (xa1, 2, (1, 1))],
        [(bm, 0, (0, 3)), (bm, 2, (1, 3)), (bp, 0, (0, 1)), (bp, 2, (1, 1))],
        so_far,
    )
    part = couple(
        place,
        tile_rows,
        tile_slabs,
        tile_count,
        inverse_panels,
        inv_par,
        [(xa2, 0, (1, 2))],
        [(b2, 0, (0, 2)), (xb2, 0, (1, 2))],
        so_far,
        tiles,
    )
    spread = lax.all_to_all(part.reshape(4096, SLAB_W), CHIPS, 0, 0, tiled=True)
    total = spread.reshape(64, 2, 32, SLAB_W).astype(jnp.float32).sum(axis=0)
    held = jnp.where(c == 0, total[0], total[1])
    got = moved(jnp.where(c == 0, total[1], total[0]), dc=1)
    coupling = jnp.concatenate(
        [jnp.where(c == 0, held, got), jnp.where(c == 0, got, held)], axis=1
    )
    earlier = earlier_term(earlier_panels, used_panels, (xh, z, c))
    return base_slab - coupling - earlier


def solution(mesh):
    split = jax.sharding.Mesh(mesh.devices.reshape(4, 2, 2, 4, 2), AXES)
    scen, intr = ("y", "xl"), ("xh", "z", "c")
    return jax.shard_map(
        on_device,
        mesh=split,
        in_specs=(
            P(scen, intr, None),
            P(scen, intr, None),
            P(scen, None, intr, None),
            P(scen, None),
            P(scen, None),
            P(scen),
            P(AXES, None),
            P(None, AXES, None),
            P(),
        ),
        out_specs=P(AXES, None),
        check_vma=False,
    )
```

```python
import functools

import jax
import jax.numpy as jnp
from jax import lax
from jax.experimental import pallas as pl
from jax.experimental.pallas import tpu as pltpu
from jax.sharding import PartitionSpec as P


COLS = 512
SLAB_W = 256
TILE = 128
LIST = 16
NTILE = 32
HERE = 4
ROWS_HERE = 256
CHIP_ROWS = 512
BATCH = 4
AXES = ("y", "xl", "xh", "z", "c")
CHIPS = ("y", "xl", "xh", "z")


def device_at(x, y, z, c):
    return (((y * 2 + x % 2) * 2 + x // 2) * 4 + z) * 2 + c


def everyone():
    return [(x, y, z, c) for x in range(4) for y in range(4) for z in range(4) for c in range(2)]


def moved(array, dx=0, dy=0, dz=0, dc=0):
    pairs = [
        (device_at(x, y, z, c), device_at((x + dx) % 4, (y + dy) % 4, (z + dz) % 4, (c + dc) % 2))
        for x, y, z, c in everyone()
    ]
    return lax.ppermute(array, AXES, sorted(pairs))


def sent(array, goes):
    pairs = []
    for x, y, z, c in everyone():
        for target in goes(x, y, z, c):
            pairs.append((device_at(x, y, z, c), device_at(*target)))
    return lax.ppermute(array, AXES, sorted(pairs))


def chip_of(place, where):
    far, shift = where
    return lax.rem(place[0] + far, 2) * 4 + lax.rem(place[1] + shift, 4)


def stage_specs(group_a, group_b):
    slots = max(len(group_a), len(group_b))
    block_specs = [
        pl.BlockSpec(
            (1, CHIP_ROWS, SLAB_W),
            functools.partial(lambda o, s, p, *_: (jnp.minimum(s, 1) + o, 0, 0), offset),
        )
        for _, offset, _ in group_a
    ] + [
        pl.BlockSpec(
            (1, CHIP_ROWS, SLAB_W),
            functools.partial(lambda o, s, p, *_: (jnp.maximum(s - 2, 0) + o, 0, 0), offset),
        )
        for _, offset, _ in group_b
    ]

    def columns(i, s, p, *_):
        at_a = chip_of(p, group_a[min(i, len(group_a) - 1)][2])
        at_b = chip_of(p, group_b[min(i, len(group_b) - 1)][2])
        return (s, 0, jnp.where(s < 2, at_a, at_b))

    inverse_specs = [
        pl.BlockSpec((1, ROWS_HERE, CHIP_ROWS), functools.partial(columns, i)) for i in range(slots)
    ]
    return block_specs, inverse_specs


def added(inv_own, inv_par, blocks):
    total = None
    for own, par, block in zip(inv_own, inv_par, blocks):
        left = jnp.concatenate([own[0], par[0]], axis=0)
        term = jnp.dot(left, block[0], preferred_element_type=jnp.float32)
        total = term if total is None else total + term
    return total


def stage_body(count_a, count_b, has_sum, place, *refs):
    s = pl.program_id(0)
    slots = max(count_a, count_b)
    blocks = refs[: count_a + count_b]
    own = refs[count_a + count_b : count_a + count_b + slots]
    par = refs[count_a + count_b + slots : count_a + count_b + 2 * slots]
    out = refs[-1]
    for here, group, count in ((s < 2, blocks[:count_a], count_a), (s >= 2, blocks[count_a:], count_b)):

        @pl.when(here)
        def _():
            total = added(own[:count], par[:count], group)
            if has_sum:
                total = total + refs[-2][0]
            out[0] = total


def stage(place, inv_own, inv_par, group_a, group_b, so_far=None):
    block_specs, inverse_specs = stage_specs(group_a, group_b)
    sum_spec = pl.BlockSpec((1, CHIP_ROWS, SLAB_W), lambda s, p: (s, 0, 0))
    slots = len(inverse_specs)
    units = 2 * (len(group_a) + len(group_b))
    return pl.pallas_call(
        functools.partial(stage_body, len(group_a), len(group_b), so_far is not None),
        out_shape=jax.ShapeDtypeStruct((HERE, CHIP_ROWS, SLAB_W), jnp.float32),
        grid_spec=pltpu.PrefetchScalarGridSpec(
            num_scalar_prefetch=1,
            grid=(HERE,),
            in_specs=block_specs
            + inverse_specs * 2
            + ([] if so_far is None else [sum_spec]),
            out_specs=sum_spec,
        ),
        cost_estimate=pl.CostEstimate(
            flops=units * 2 * 512 * 512 * 256, bytes_accessed=units << 19, transcendentals=0
        ),
    )(
        place,
        *[array for array, _, _ in group_a + group_b],
        *([inv_own] * slots),
        *([inv_par] * slots),
        *([] if so_far is None else [so_far]),
    )


def prepare_body(slabs, counts, place, t_own, t_par, out):
    s = pl.program_id(0)

    def step(l, found):
        hit = slabs[s, l] == place[2]

        @pl.when(hit)
        def _():
            out[0, found, :, :ROWS_HERE] = t_own[0, l].T
            out[0, found, :, ROWS_HERE:] = t_par[0, l].T

        return found + hit.astype(jnp.int32)

    lax.fori_loop(0, counts[s], step, jnp.int32(0))


def prepare(slabs, counts, place, t_own, t_par):
    tile_spec = pl.BlockSpec((1, LIST, ROWS_HERE, TILE), lambda s, *_: (s, 0, 0, 0))
    return pl.pallas_call(
        prepare_body,
        out_shape=jax.ShapeDtypeStruct((HERE, LIST, TILE, CHIP_ROWS), jnp.bfloat16),
        grid_spec=pltpu.PrefetchScalarGridSpec(
            num_scalar_prefetch=3,
            grid=(HERE,),
            in_specs=[tile_spec, tile_spec],
            out_specs=pl.BlockSpec((1, LIST, TILE, CHIP_ROWS), lambda s, *_: (s, 0, 0, 0)),
        ),
        cost_estimate=pl.CostEstimate(flops=1 << 20, bytes_accessed=16 << 20, transcendentals=0),
        name="prepare",
    )(slabs, counts, place, t_own, t_par)


def couple_body(count_a, count_b, place, rows, slabs, counts, *refs):
    s = pl.program_id(0)
    slots = max(count_a, count_b)
    blocks = refs[: count_a + count_b]
    own = refs[count_a + count_b : count_a + count_b + slots]
    par = refs[count_a + count_b + slots : count_a + count_b + 2 * slots]
    so_far, tiles, out, acc, applied, held, found_rows, found_count, sems = refs[-9:]

    def batches(at):
        return (found_count[at] + BATCH - 1) // BATCH

    def copy(at, b):
        part = pl.ds(b * BATCH, BATCH)
        return pltpu.make_async_copy(tiles.at[at, part], held.at[at, part], sems.at[at])

    @pl.when(s == 0)
    def _():
        for at in range(HERE):

            def look(l, found, at=at):
                hit = slabs[at, l] == place[2]

                @pl.when(hit)
                def _():
                    found_rows[at, found] = rows[at, l]

                return found + hit.astype(jnp.int32)

            found_count[at] = lax.fori_loop(0, counts[at], look, jnp.int32(0))

            def fetch(b, carry, at=at):
                copy(at, b).start()
                return carry

            lax.fori_loop(0, batches(at), fetch, 0)
        acc[...] = jnp.zeros_like(acc)

    for here, group, count in ((s < 2, blocks[:count_a], count_a), (s >= 2, blocks[count_a:], count_b)):

        @pl.when(here)
        def _():
            total = added(own[:count], par[:count], group) + so_far[0]
            applied[...] = total.astype(jnp.bfloat16)

    def landed(b, carry):
        copy(s, b).wait()
        return carry

    lax.fori_loop(0, batches(s), landed, 0)
    found = found_count[s]

    def step(b, carry):
        left = held[s, pl.ds(b * BATCH, BATCH)].reshape(BATCH * TILE, CHIP_ROWS)
        term = jnp.dot(left, applied[...], preferred_element_type=jnp.float32)
        for j in range(BATCH):

            @pl.when(b * BATCH + j < found)
            def _():
                acc[found_rows[s, b * BATCH + j]] += term[j * TILE : (j + 1) * TILE]

        return carry

    lax.fori_loop(0, batches(s), step, 0)

    @pl.when(s == HERE - 1)
    def _():
        out[...] = acc[...].astype(jnp.bfloat16)


def couple(place, rows, slabs, counts, inv_own, inv_par, group_a, group_b, so_far, tiles):
    block_specs, inverse_specs = stage_specs(group_a, group_b)
    slots = len(inverse_specs)
    return pl.pallas_call(
        functools.partial(couple_body, len(group_a), len(group_b)),
        out_shape=jax.ShapeDtypeStruct((NTILE, TILE, SLAB_W), jnp.bfloat16),
        grid_spec=pltpu.PrefetchScalarGridSpec(
            num_scalar_prefetch=4,
            grid=(HERE,),
            in_specs=block_specs
            + inverse_specs * 2
            + [
                pl.BlockSpec((1, CHIP_ROWS, SLAB_W), lambda s, *_: (s, 0, 0)),
                pl.BlockSpec(memory_space=pl.ANY),
            ],
            out_specs=pl.BlockSpec((NTILE, TILE, SLAB_W), lambda s, *_: (0, 0, 0)),
            scratch_shapes=[
                pltpu.VMEM((NTILE, TILE, SLAB_W), jnp.float32),
                pltpu.VMEM((CHIP_ROWS, SLAB_W), jnp.bfloat16),
                pltpu.VMEM((HERE, LIST, TILE, CHIP_ROWS), jnp.bfloat16),
                pltpu.SMEM((HERE, LIST), jnp.int32),
                pltpu.SMEM((HERE,), jnp.int32),
                pltpu.SemaphoreType.DMA((HERE,)),
            ],
        ),
        cost_estimate=pl.CostEstimate(flops=3 << 30, bytes_accessed=16 << 20, transcendentals=0),
        name="couple",
    )(
        place,
        rows,
        slabs,
        counts,
        *[array for array, _, _ in group_a + group_b],
        *([inv_own] * slots),
        *([inv_par] * slots),
        so_far,
        tiles,
    )


def earlier_term(earlier_panels, used_panels, where):
    y = lax.axis_index("y")
    xl = lax.axis_index("xl")
    xh, z, c = where
    chosen = earlier_panels[used_panels]
    got = sent(chosen, lambda x, y, z, c: [(x, 1, z, c)] if y == 0 and x % 2 == 0 else [])
    top = jnp.where(y == 1, got, chosen)
    got = sent(top, lambda x, y, z, c: [(x, 3 - y, z, c)] if y < 2 and x % 2 == 0 else [])
    top = jnp.where(y >= 2, got, top)
    got = sent(top, lambda x, y, z, c: [(x + 1, y, z, c)] if x % 2 == 0 else [])
    top = jnp.where(xl == 1, got, top)
    other = moved(top, dc=1)
    pair = jnp.stack([jnp.where(c == 0, top, other), jnp.where(c == 0, other, top)])
    line = jnp.stack([pair, moved(pair, dz=-1), moved(pair, dz=2), moved(pair, dz=1)])
    far = moved(line, dx=2)
    plane = jnp.stack([line, far])
    at_x = lax.rem(jnp.arange(2, dtype=jnp.int32) + xh, 2)
    at_z = lax.rem(jnp.arange(4, dtype=jnp.int32) + 4 - z, 4)
    order = (at_x[:, None] * 4 + at_z[None, :]).reshape(8)
    ordered = plane.reshape(8, 2, 4, 32, TILE)[order]
    top_rows = ordered.reshape(16, 4, 32, TILE).transpose(1, 0, 2, 3).reshape(4, COLS, TILE)
    return jnp.einsum("prt,pct->rc", chosen, top_rows, preferred_element_type=jnp.float32)


def on_device(
    inverse_panels,
    border_columns,
    border_tiles,
    tile_rows,
    tile_slabs,
    tile_count,
    base_slab,
    earlier_panels,
    used_panels,
):
    xh = lax.axis_index("xh")
    z = lax.axis_index("z")
    c = lax.axis_index("c")
    place = jnp.stack([xh, z, c]).astype(jnp.int32)

    low, high = border_columns[:, :, :SLAB_W], border_columns[:, :, SLAB_W:]
    got = moved(jnp.where(c == 0, high, low), dc=1)
    mine = jnp.where(
        c == 0, jnp.concatenate([low, got], axis=1), jnp.concatenate([got, high], axis=1)
    )
    inv_par = moved(inverse_panels, dc=1)
    t_par = moved(border_tiles, dc=1)

    a0, b0 = mine[:2], mine[2:]
    bx = moved(b0, dx=2)
    ap = moved(a0, dz=-1)
    am = moved(a0, dz=1)
    xa0 = moved(a0, dx=2)
    bb = jnp.concatenate([b0, bx], axis=0)
    bp = moved(bb, dz=-1)
    bm = moved(bb, dz=1)
    a2 = moved(am, dz=1)
    xa1 = moved(jnp.concatenate([am, ap], axis=0), dx=2)
    xa2 = moved(a2, dx=2)
    b2 = moved(bp, dz=-1)

    tiles = prepare(tile_slabs, tile_count, place, border_tiles, t_par)
    so_far = stage(
        place,
        inverse_panels,
        inv_par,
        [
            (a0, 0, (0, 0)),
            (am, 0, (0, 3)),
            (ap, 0, (0, 1)),
            (a2, 0, (0, 2)),
            (xa0, 0, (1, 0)),
            (xa1, 0, (1, 3)),
            (xa1, 2, (1, 1)),
        ],
        [
            (bb, 0, (0, 0)),
            (bb, 2, (1, 0)),
            (bm, 0, (0, 3)),
            (bm, 2, (1, 3)),
            (bp, 0, (0, 1)),
            (bp, 2, (1, 1)),
        ],
    )
    part = couple(
        place,
        tile_rows,
        tile_slabs,
        tile_count,
        inverse_panels,
        inv_par,
        [(xa2, 0, (1, 2))],
        [(b2, 0, (0, 2)), (b2, 2, (1, 2))],
        so_far,
        tiles,
    )
    spread = lax.all_to_all(part.reshape(4096, SLAB_W), CHIPS, 0, 0, tiled=True)
    total = spread.reshape(64, 2, 32, SLAB_W).astype(jnp.float32).sum(axis=0)
    held = jnp.where(c == 0, total[0], total[1])
    got = moved(jnp.where(c == 0, total[1], total[0]), dc=1)
    coupling = jnp.concatenate(
        [jnp.where(c == 0, held, got), jnp.where(c == 0, got, held)], axis=1
    )
    earlier = earlier_term(earlier_panels, used_panels, (xh, z, c))
    return base_slab - coupling - earlier


def solution(mesh):
    split = jax.sharding.Mesh(mesh.devices.reshape(4, 2, 2, 4, 2), AXES)
    scen, intr = ("y", "xl"), ("xh", "z", "c")
    return jax.shard_map(
        on_device,
        mesh=split,
        in_specs=(
            P(scen, intr, None),
            P(scen, intr, None),
            P(scen, None, intr, None),
            P(scen, None),
            P(scen, None),
            P(scen),
            P(AXES, None),
            P(None, AXES, None),
            P(),
        ),
        out_specs=P(AXES, None),
        check_vma=False,
    )
```

```python
import functools

import jax
import jax.numpy as jnp
from jax import lax
from jax.experimental import pallas as pl
from jax.experimental.pallas import tpu as pltpu
from jax.sharding import PartitionSpec as P


COLS = 512
SLAB_W = 256
TILE = 128
LIST = 16
NTILE = 32
HERE = 4
ROWS_HERE = 256
CHIP_ROWS = 512
BATCH = 4
AXES = ("y", "xl", "xh", "z", "c")
CHIPS = ("y", "xl", "xh", "z")


def device_at(x, y, z, c):
    return (((y * 2 + x % 2) * 2 + x // 2) * 4 + z) * 2 + c


def everyone():
    return [(x, y, z, c) for x in range(4) for y in range(4) for z in range(4) for c in range(2)]


def moved(array, dx=0, dy=0, dz=0, dc=0):
    pairs = [
        (device_at(x, y, z, c), device_at((x + dx) % 4, (y + dy) % 4, (z + dz) % 4, (c + dc) % 2))
        for x, y, z, c in everyone()
    ]
    return lax.ppermute(array, AXES, sorted(pairs))


def sent(array, goes):
    pairs = []
    for x, y, z, c in everyone():
        for target in goes(x, y, z, c):
            pairs.append((device_at(x, y, z, c), device_at(*target)))
    return lax.ppermute(array, AXES, sorted(pairs))


def picked(table, s):
    value = table[0]
    for k in range(1, HERE):
        value = jnp.where(s == k, table[k], value)
    return value


def layout(groups):
    operands, tables, uses = [], [], []
    for s, group in enumerate(groups):
        mine = []
        for array, block, _ in group:
            for at, operand in enumerate(operands):
                if operand is array and s not in tables[at]:
                    break
            else:
                at = len(operands)
                operands.append(array)
                tables.append({})
            tables[at][s] = block
            mine.append(at)
        uses.append(mine)
    specs = []
    for table in tables:
        full = [table.get(s, table[min(table, key=lambda k: abs(k - s))]) for s in range(HERE)]
        specs.append(
            pl.BlockSpec(
                (1, CHIP_ROWS, SLAB_W),
                functools.partial(lambda full, s, *_: (picked(full, s), 0, 0), full),
            )
        )
    slots = max(len(group) for group in groups)

    def columns(i, s, place, *_):
        wheres = [group[min(i, len(group) - 1)][2] for group in groups]
        far = picked([where[0] for where in wheres], s)
        shift = picked([where[1] for where in wheres], s)
        return (s, 0, lax.rem(place[0] + far, 2) * 4 + lax.rem(place[1] + shift, 4))

    inverse = [
        pl.BlockSpec((1, ROWS_HERE, CHIP_ROWS), functools.partial(columns, i)) for i in range(slots)
    ]
    return operands, specs, inverse, uses


def added(own, par, blocks, mine):
    total = None
    for i, at in enumerate(mine):
        left = jnp.concatenate([own[i][0], par[i][0]], axis=0)
        term = jnp.dot(left, blocks[at][0], preferred_element_type=jnp.float32)
        total = term if total is None else total + term
    return total


def split_refs(refs, count, slots):
    blocks, rest = refs[:count], refs[count:]
    return blocks, rest[:slots], rest[slots : 2 * slots], rest[2 * slots :]


def stage_body(count, slots, uses, has_sum, place, *refs):
    s = pl.program_id(0)
    blocks, own, par, rest = split_refs(refs, count, slots)
    for k in range(HERE):

        @pl.when(s == k)
        def _():
            total = added(own, par, blocks, uses[k])
            if has_sum:
                total = total + rest[0][0]
            rest[-1][0] = total


def stage(place, inv_own, inv_par, groups, so_far=None):
    operands, specs, inverse, uses = layout(groups)
    sum_spec = pl.BlockSpec((1, CHIP_ROWS, SLAB_W), lambda s, p: (s, 0, 0))
    slots = len(inverse)
    units = sum(len(group) for group in groups)
    return pl.pallas_call(
        functools.partial(stage_body, len(operands), slots, uses, so_far is not None),
        out_shape=jax.ShapeDtypeStruct((HERE, CHIP_ROWS, SLAB_W), jnp.float32),
        grid_spec=pltpu.PrefetchScalarGridSpec(
            num_scalar_prefetch=1,
            grid=(HERE,),
            in_specs=specs + inverse * 2 + ([] if so_far is None else [sum_spec]),
            out_specs=sum_spec,
        ),
        cost_estimate=pl.CostEstimate(
            flops=units * 2 * 512 * 512 * 256, bytes_accessed=units << 19, transcendentals=0
        ),
    )(
        place,
        *operands,
        *([inv_own] * slots),
        *([inv_par] * slots),
        *([] if so_far is None else [so_far]),
    )


def prepare_body(slabs, counts, place, t_own, t_par, out):
    s = pl.program_id(0)

    def step(l, found):
        hit = slabs[s, l] == place[2]

        @pl.when(hit)
        def _():
            out[0, found, :, :ROWS_HERE] = t_own[0, l].T
            out[0, found, :, ROWS_HERE:] = t_par[0, l].T

        return found + hit.astype(jnp.int32)

    lax.fori_loop(0, counts[s], step, jnp.int32(0))


def prepare(slabs, counts, place, t_own, t_par):
    tile_spec = pl.BlockSpec((1, LIST, ROWS_HERE, TILE), lambda s, *_: (s, 0, 0, 0))
    return pl.pallas_call(
        prepare_body,
        out_shape=jax.ShapeDtypeStruct((HERE, LIST, TILE, CHIP_ROWS), jnp.bfloat16),
        grid_spec=pltpu.PrefetchScalarGridSpec(
            num_scalar_prefetch=3,
            grid=(HERE,),
            in_specs=[tile_spec, tile_spec],
            out_specs=pl.BlockSpec((1, LIST, TILE, CHIP_ROWS), lambda s, *_: (s, 0, 0, 0)),
        ),
        cost_estimate=pl.CostEstimate(flops=1 << 20, bytes_accessed=16 << 20, transcendentals=0),
        name="prepare",
    )(slabs, counts, place, t_own, t_par)


def couple_body(count, slots, uses, place, rows, slabs, counts, *refs):
    s = pl.program_id(0)
    blocks, own, par, rest = split_refs(refs, count, slots)
    so_far, tiles, out, acc, applied, held, found_rows, found_count, sems = rest

    def batches(at):
        return (found_count[at] + BATCH - 1) // BATCH

    def copy(at, b):
        part = pl.ds(b * BATCH, BATCH)
        return pltpu.make_async_copy(tiles.at[at, part], held.at[at, part], sems.at[at])

    @pl.when(s == 0)
    def _():
        for at in range(HERE):

            def look(l, found, at=at):
                hit = slabs[at, l] == place[2]

                @pl.when(hit)
                def _():
                    found_rows[at, found] = rows[at, l]

                return found + hit.astype(jnp.int32)

            found_count[at] = lax.fori_loop(0, counts[at], look, jnp.int32(0))

            def fetch(b, carry, at=at):
                copy(at, b).start()
                return carry

            lax.fori_loop(0, batches(at), fetch, 0)
        acc[...] = jnp.zeros_like(acc)

    for k in range(HERE):

        @pl.when(s == k)
        def _():
            total = added(own, par, blocks, uses[k]) + so_far[0]
            applied[...] = total.astype(jnp.bfloat16)

    def landed(b, carry):
        copy(s, b).wait()
        return carry

    lax.fori_loop(0, batches(s), landed, 0)
    found = found_count[s]

    def step(b, carry):
        left = held[s, pl.ds(b * BATCH, BATCH)].reshape(BATCH * TILE, CHIP_ROWS)
        term = jnp.dot(left, applied[...], preferred_element_type=jnp.float32)
        for j in range(BATCH):

            @pl.when(b * BATCH + j < found)
            def _():
                acc[found_rows[s, b * BATCH + j]] += term[j * TILE : (j + 1) * TILE]

        return carry

    lax.fori_loop(0, batches(s), step, 0)

    @pl.when(s == HERE - 1)
    def _():
        out[...] = acc[...].astype(jnp.bfloat16)


def couple(place, rows, slabs, counts, inv_own, inv_par, groups, so_far, tiles):
    operands, specs, inverse, uses = layout(groups)
    slots = len(inverse)
    return pl.pallas_call(
        functools.partial(couple_body, len(operands), slots, uses),
        out_shape=jax.ShapeDtypeStruct((NTILE, TILE, SLAB_W), jnp.bfloat16),
        grid_spec=pltpu.PrefetchScalarGridSpec(
            num_scalar_prefetch=4,
            grid=(HERE,),
            in_specs=specs
            + inverse * 2
            + [
                pl.BlockSpec((1, CHIP_ROWS, SLAB_W), lambda s, *_: (s, 0, 0)),
                pl.BlockSpec(memory_space=pl.ANY),
            ],
            out_specs=pl.BlockSpec((NTILE, TILE, SLAB_W), lambda s, *_: (0, 0, 0)),
            scratch_shapes=[
                pltpu.VMEM((NTILE, TILE, SLAB_W), jnp.float32),
                pltpu.VMEM((CHIP_ROWS, SLAB_W), jnp.bfloat16),
                pltpu.VMEM((HERE, LIST, TILE, CHIP_ROWS), jnp.bfloat16),
                pltpu.SMEM((HERE, LIST), jnp.int32),
                pltpu.SMEM((HERE,), jnp.int32),
                pltpu.SemaphoreType.DMA((HERE,)),
            ],
        ),
        cost_estimate=pl.CostEstimate(flops=3 << 30, bytes_accessed=16 << 20, transcendentals=0),
        name="couple",
    )(
        place,
        rows,
        slabs,
        counts,
        *operands,
        *([inv_own] * slots),
        *([inv_par] * slots),
        so_far,
        tiles,
    )


def earlier_term(earlier_panels, used_panels, where):
    y = lax.axis_index("y")
    xl = lax.axis_index("xl")
    xh, z, c = where
    chosen = earlier_panels[used_panels]
    got = sent(chosen, lambda x, y, z, c: [(x, 1, z, c)] if y == 0 and x % 2 == 0 else [])
    top = jnp.where(y == 1, got, chosen)
    got = sent(top, lambda x, y, z, c: [(x, 3 - y, z, c)] if y < 2 and x % 2 == 0 else [])
    top = jnp.where(y >= 2, got, top)
    got = sent(top, lambda x, y, z, c: [(x + 1, y, z, c)] if x % 2 == 0 else [])
    top = jnp.where(xl == 1, got, top)
    other = moved(top, dc=1)
    pair = jnp.stack([jnp.where(c == 0, top, other), jnp.where(c == 0, other, top)])
    line = jnp.stack([pair, moved(pair, dz=-1), moved(pair, dz=2), moved(pair, dz=1)])
    far = moved(line, dx=2)
    plane = jnp.stack([line, far])
    at_x = lax.rem(jnp.arange(2, dtype=jnp.int32) + xh, 2)
    at_z = lax.rem(jnp.arange(4, dtype=jnp.int32) + 4 - z, 4)
    order = (at_x[:, None] * 4 + at_z[None, :]).reshape(8)
    ordered = plane.reshape(8, 2, 4, 32, TILE)[order]
    top_rows = ordered.reshape(16, 4, 32, TILE).transpose(1, 0, 2, 3).reshape(4, COLS, TILE)
    return jnp.einsum("prt,pct->rc", chosen, top_rows, preferred_element_type=jnp.float32)


def on_device(
    inverse_panels,
    border_columns,
    border_tiles,
    tile_rows,
    tile_slabs,
    tile_count,
    base_slab,
    earlier_panels,
    used_panels,
):
    xh = lax.axis_index("xh")
    z = lax.axis_index("z")
    c = lax.axis_index("c")
    place = jnp.stack([xh, z, c]).astype(jnp.int32)

    low, high = border_columns[:, :, :SLAB_W], border_columns[:, :, SLAB_W:]
    got = moved(jnp.where(c == 0, high, low), dc=1)
    mine = jnp.where(
        c == 0, jnp.concatenate([low, got], axis=1), jnp.concatenate([got, high], axis=1)
    )
    inv_par = moved(inverse_panels, dc=1)
    t_par = moved(border_tiles, dc=1)

    a0, b0 = mine[:2], mine[2:]
    bx = moved(b0, dx=2)
    ap = moved(a0, dz=-1)
    am = moved(a0, dz=1)
    xa0 = moved(a0, dx=2)
    bb = jnp.concatenate([b0, bx], axis=0)
    bp = moved(bb, dz=-1)
    bm = moved(bb, dz=1)
    a2 = moved(am, dz=1)
    xa1 = moved(jnp.concatenate([am, ap], axis=0), dx=2)
    xa2 = moved(a2, dx=2)
    b2a = moved(bp[:3], dz=-1)
    b2b = moved(bm[3:], dz=1)

    tiles = prepare(tile_slabs, tile_count, place, border_tiles, t_par)
    near, far = 0, 1
    so_far = stage(
        place,
        inverse_panels,
        inv_par,
        [
            [
                (a0, g, (near, 0)),
                (am, g, (near, 3)),
                (ap, g, (near, 1)),
                (a2, g, (near, 2)),
                (xa0, g, (far, 0)),
            ]
            for g in range(2)
        ]
        + [
            [
                (bb, g, (near, 0)),
                (bb, 2 + g, (far, 0)),
                (bp, g, (near, 1)),
                (bp, 2 + g, (far, 1)),
            ]
            for g in range(2)
        ],
    )
    so_far = stage(
        place,
        inverse_panels,
        inv_par,
        [[(xa1, g, (far, 3)), (xa1, 2 + g, (far, 1))] for g in range(2)]
        + [[(bm, g, (near, 3)), (bm, 2 + g, (far, 3))] for g in range(2)],
        so_far,
    )
    part = couple(
        place,
        tile_rows,
        tile_slabs,
        tile_count,
        inverse_panels,
        inv_par,
        [
            [(xa2, 0, (far, 2))],
            [(xa2, 1, (far, 2))],
            [(b2a, 0, (near, 2)), (b2a, 2, (far, 2))],
            [(b2a, 1, (near, 2)), (b2b, 0, (far, 2))],
        ],
        so_far,
        tiles,
    )
    spread = lax.all_to_all(part.reshape(4096, SLAB_W), CHIPS, 0, 0, tiled=True)
    total = spread.reshape(64, 2, 32, SLAB_W).astype(jnp.float32).sum(axis=0)
    held = jnp.where(c == 0, total[0], total[1])
    got = moved(jnp.where(c == 0, total[1], total[0]), dc=1)
    coupling = jnp.concatenate(
        [jnp.where(c == 0, held, got), jnp.where(c == 0, got, held)], axis=1
    )
    earlier = earlier_term(earlier_panels, used_panels, (xh, z, c))
    return base_slab - coupling - earlier


def solution(mesh):
    split = jax.sharding.Mesh(mesh.devices.reshape(4, 2, 2, 4, 2), AXES)
    scen, intr = ("y", "xl"), ("xh", "z", "c")
    return jax.shard_map(
        on_device,
        mesh=split,
        in_specs=(
            P(scen, intr, None),
            P(scen, intr, None),
            P(scen, None, intr, None),
            P(scen, None),
            P(scen, None),
            P(scen),
            P(AXES, None),
            P(None, AXES, None),
            P(),
        ),
        out_specs=P(AXES, None),
        check_vma=False,
    )
```

```python
import functools

import jax
import jax.numpy as jnp
from jax import lax
from jax.experimental import pallas as pl
from jax.experimental.pallas import tpu as pltpu
from jax.sharding import PartitionSpec as P


COLS = 512
SLAB_W = 256
TILE = 128
LIST = 16
NTILE = 32
HERE = 4
ROWS_HERE = 256
CHIP_ROWS = 512
BATCH = 2
AXES = ("y", "xl", "xh", "z", "c")
CHIPS = ("y", "xl", "xh", "z")


def device_at(x, y, z, c):
    return (((y * 2 + x % 2) * 2 + x // 2) * 4 + z) * 2 + c


def everyone():
    return [(x, y, z, c) for x in range(4) for y in range(4) for z in range(4) for c in range(2)]


def moved(array, dx=0, dy=0, dz=0, dc=0):
    pairs = [
        (device_at(x, y, z, c), device_at((x + dx) % 4, (y + dy) % 4, (z + dz) % 4, (c + dc) % 2))
        for x, y, z, c in everyone()
    ]
    return lax.ppermute(array, AXES, sorted(pairs))


ANY = pl.BlockSpec(memory_space=pl.ANY)
SCALAR = pl.BlockSpec(memory_space=pltpu.SMEM)


def layout(groups):
    operands, plan = [], []
    for s, group in enumerate(groups):
        for array, block, where in group:
            at = next((i for i, operand in enumerate(operands) if operand is array), len(operands))
            if at == len(operands):
                operands.append(array)
            plan.append((s, at, block, where))
    return operands, plan


def fetches(plan, place, blocks, inv_own, inv_par, held, turned, sems):
    units = []
    for n, (s, at, block, (far, shift)) in enumerate(plan):
        chip = lax.rem(place[0] + far, 2) * 4 + lax.rem(place[1] + shift, 4)
        columns = pl.ds(pl.multiple_of(chip * CHIP_ROWS, CHIP_ROWS), CHIP_ROWS)
        upper, lower = pl.ds(0, ROWS_HERE), pl.ds(ROWS_HERE, ROWS_HERE)
        units.append(
            [
                pltpu.make_async_copy(blocks[at].at[block], held.at[n], sems.at[n]),
                pltpu.make_async_copy(inv_own.at[s, :, columns], turned.at[n, upper], sems.at[n]),
                pltpu.make_async_copy(inv_par.at[s, :, columns], turned.at[n, lower], sems.at[n]),
            ]
        )
    return units


def added(s, plan, units, held, turned):
    total = None
    for n, unit in enumerate(plan):
        if unit[0] == s:
            for copy in units[n]:
                copy.wait()
            term = jnp.dot(turned[n], held[n], preferred_element_type=jnp.float32)
            total = term if total is None else total + term
    return total


def stage_body(plan, count, has_sum, place, *refs):
    blocks, (inv_own, inv_par, *refs) = refs[:count], refs[count:]
    so_far, refs = (refs[0], refs[1:]) if has_sum else (None, refs)
    out, held, turned, kept, unit_sems, sum_sems, out_sems = refs
    units = fetches(plan, place, blocks, inv_own, inv_par, held, turned, unit_sems)
    sums = []
    if has_sum:
        sums = [
            pltpu.make_async_copy(so_far.at[s], kept.at[s], sum_sems.at[s]) for s in range(HERE)
        ]
    for s in range(HERE):
        for n, unit in enumerate(plan):
            if unit[0] == s:
                for copy in units[n]:
                    copy.start()
        if has_sum:
            sums[s].start()
    writes = []
    for s in range(HERE):
        total = added(s, plan, units, held, turned)
        if has_sum:
            sums[s].wait()
            total = total + kept[s]
        kept[s] = total
        write = pltpu.make_async_copy(kept.at[s], out.at[s], out_sems.at[s])
        write.start()
        writes.append(write)
    for write in writes:
        write.wait()


def stage(place, inv_own, inv_par, groups, so_far=None):
    operands, plan = layout(groups)
    units = len(plan)
    has_sum = so_far is not None
    return pl.pallas_call(
        functools.partial(stage_body, plan, len(operands), has_sum),
        out_shape=jax.ShapeDtypeStruct((HERE, CHIP_ROWS, SLAB_W), jnp.float32),
        in_specs=[SCALAR] + [ANY] * (len(operands) + 2 + has_sum),
        out_specs=ANY,
        scratch_shapes=[
            pltpu.VMEM((units, CHIP_ROWS, SLAB_W), jnp.bfloat16),
            pltpu.VMEM((units, CHIP_ROWS, CHIP_ROWS), jnp.bfloat16),
            pltpu.VMEM((HERE, CHIP_ROWS, SLAB_W), jnp.float32),
            pltpu.SemaphoreType.DMA((units,)),
            pltpu.SemaphoreType.DMA((HERE,)),
            pltpu.SemaphoreType.DMA((HERE,)),
        ],
        cost_estimate=pl.CostEstimate(
            flops=units * 2 * 512 * 512 * 256, bytes_accessed=units << 19, transcendentals=0
        ),
    )(place, *operands, inv_own, inv_par, *([so_far] if has_sum else []))


def couple_body(plan, count, place, rows, slabs, counts, *refs):
    blocks, refs = refs[:count], refs[count:]
    inv_own, inv_par, so_far, t_own, t_par, out, held, turned, kept, tiles, acc, rounded = refs[:12]
    applied, found_rows, found_count, unit_sems, sum_sems, tile_sems, out_sems = refs[12:]
    units = fetches(plan, place, blocks, inv_own, inv_par, held, turned, unit_sems)
    sums = [pltpu.make_async_copy(so_far.at[s], kept.at[s], sum_sems.at[s]) for s in range(HERE)]

    def tile_copies(s, l, slot):
        upper, lower = pl.ds(0, ROWS_HERE), pl.ds(ROWS_HERE, ROWS_HERE)
        return (
            pltpu.make_async_copy(t_own.at[s, l], tiles.at[s, slot, upper], tile_sems.at[s]),
            pltpu.make_async_copy(t_par.at[s, l], tiles.at[s, slot, lower], tile_sems.at[s]),
        )

    for s in range(HERE):
        for n, unit in enumerate(plan):
            if unit[0] == s:
                for copy in units[n]:
                    copy.start()
        sums[s].start()

        def look(l, found, s=s):
            hit = slabs[s, l] == place[2]

            @pl.when(hit)
            def _():
                found_rows[s, found] = rows[s, l]
                for copy in tile_copies(s, l, found):
                    copy.start()

            return found + hit.astype(jnp.int32)

        found_count[s] = lax.fori_loop(0, counts[s], look, jnp.int32(0))
    acc[...] = jnp.zeros_like(acc)
    for s in range(HERE):
        total = added(s, plan, units, held, turned)
        sums[s].wait()
        applied[...] = (total + kept[s]).astype(jnp.bfloat16)
        found = found_count[s]

        def landed(slot, carry, s=s):
            for copy in tile_copies(s, 0, slot):
                copy.wait()
            return carry

        lax.fori_loop(0, found, landed, 0)

        def step(b, carry, s=s, found=found):
            left = jnp.concatenate([tiles[s, b * BATCH + j].T for j in range(BATCH)], axis=0)
            term = jnp.dot(left, applied[...], preferred_element_type=jnp.float32)
            for j in range(BATCH):

                @pl.when(b * BATCH + j < found)
                def _():
                    acc[found_rows[s, b * BATCH + j]] += term[j * TILE : (j + 1) * TILE]

            return carry

        lax.fori_loop(0, (found + BATCH - 1) // BATCH, step, 0)
    writes = []
    for part in range(4):
        span = pl.ds(part * (NTILE // 4), NTILE // 4)
        rounded[span] = acc[span].astype(jnp.bfloat16)
        write = pltpu.make_async_copy(rounded.at[span], out.at[span], out_sems.at[part])
        write.start()
        writes.append(write)
    for write in writes:
        write.wait()


def couple(place, rows, slabs, counts, inv_own, inv_par, groups, so_far, t_own, t_par):
    operands, plan = layout(groups)
    units = len(plan)
    return pl.pallas_call(
        functools.partial(couple_body, plan, len(operands)),
        out_shape=jax.ShapeDtypeStruct((NTILE, TILE, SLAB_W), jnp.bfloat16),
        in_specs=[SCALAR] * 4 + [ANY] * (len(operands) + 5),
        out_specs=ANY,
        scratch_shapes=[
            pltpu.VMEM((units, CHIP_ROWS, SLAB_W), jnp.bfloat16),
            pltpu.VMEM((units, CHIP_ROWS, CHIP_ROWS), jnp.bfloat16),
            pltpu.VMEM((HERE, CHIP_ROWS, SLAB_W), jnp.float32),
            pltpu.VMEM((HERE, LIST, CHIP_ROWS, TILE), jnp.bfloat16),
            pltpu.VMEM((NTILE, TILE, SLAB_W), jnp.float32),
            pltpu.VMEM((NTILE, TILE, SLAB_W), jnp.bfloat16),
            pltpu.VMEM((CHIP_ROWS, SLAB_W), jnp.bfloat16),
            pltpu.SMEM((HERE, LIST), jnp.int32),
            pltpu.SMEM((HERE,), jnp.int32),
            pltpu.SemaphoreType.DMA((units,)),
            pltpu.SemaphoreType.DMA((HERE,)),
            pltpu.SemaphoreType.DMA((HERE,)),
            pltpu.SemaphoreType.DMA((4,)),
        ],
        cost_estimate=pl.CostEstimate(flops=3 << 30, bytes_accessed=12 << 20, transcendentals=0),
        name="couple",
    )(
        place,
        rows,
        slabs,
        counts,
        *operands,
        inv_own,
        inv_par,
        so_far,
        t_own,
        t_par,
    )


def to_all(array, axes, size):
    return lax.all_to_all(
        jnp.broadcast_to(array[None], (size, *array.shape)), axes, 0, 0, tiled=True
    )


def earlier_rows(earlier_panels, used_panels):
    chosen = earlier_panels[used_panels]
    top = to_all(chosen, ("y", "xl"), 8)[0]
    return chosen, to_all(top, ("xh", "z", "c"), 16)


def earlier_term(chosen, line):
    top_rows = line.transpose(1, 0, 2, 3).reshape(4, COLS, TILE)
    return jnp.einsum("prt,pct->rc", chosen, top_rows, preferred_element_type=jnp.float32)


def on_device(
    inverse_panels,
    border_columns,
    border_tiles,
    tile_rows,
    tile_slabs,
    tile_count,
    base_slab,
    earlier_panels,
    used_panels,
):
    xh = lax.axis_index("xh")
    z = lax.axis_index("z")
    c = lax.axis_index("c")
    place = jnp.stack([xh, z, c]).astype(jnp.int32)

    low, high = border_columns[:, :, :SLAB_W], border_columns[:, :, SLAB_W:]
    got = moved(jnp.where(c == 0, high, low), dc=1)
    mine = jnp.where(
        c == 0, jnp.concatenate([low, got], axis=1), jnp.concatenate([got, high], axis=1)
    )
    inv_par = moved(inverse_panels, dc=1)
    t_par = moved(border_tiles, dc=1)

    a0, b0 = mine[:2], mine[2:]
    bx = moved(b0, dx=2)
    ap = moved(a0, dz=-1)
    am = moved(a0, dz=1)
    xa0 = moved(a0, dx=2)
    bb = jnp.concatenate([b0, bx], axis=0)
    bp = moved(bb, dz=-1)
    bm = moved(bb, dz=1)
    a2 = moved(am, dz=1)
    xa1 = moved(jnp.concatenate([am, ap], axis=0), dx=2)
    xa2 = moved(a2, dx=2)
    b2a = moved(bp[:3], dz=-1)
    b2b = moved(bm[3:], dz=1)

    near, far = 0, 1
    so_far = stage(
        place,
        inverse_panels,
        inv_par,
        [
            [
                (a0, g, (near, 0)),
                (am, g, (near, 3)),
                (ap, g, (near, 1)),
                (a2, g, (near, 2)),
                (xa0, g, (far, 0)),
            ]
            for g in range(2)
        ]
        + [
            [
                (bb, g, (near, 0)),
                (bb, 2 + g, (far, 0)),
            ]
            for g in range(2)
        ],
    )
    so_far = stage(
        place,
        inverse_panels,
        inv_par,
        [[(xa1, g, (far, 3)), (xa1, 2 + g, (far, 1))] for g in range(2)]
        + [
            [
                (bp, g, (near, 1)),
                (bp, 2 + g, (far, 1)),
                (bm, g, (near, 3)),
                (bm, 2 + g, (far, 3)),
            ]
            for g in range(2)
        ],
        so_far,
    )
    part = couple(
        place,
        tile_rows,
        tile_slabs,
        tile_count,
        inverse_panels,
        inv_par,
        [
            [(xa2, 0, (far, 2))],
            [(xa2, 1, (far, 2))],
            [(b2a, 0, (near, 2)), (b2a, 2, (far, 2))],
            [(b2a, 1, (near, 2)), (b2b, 0, (far, 2))],
        ],
        so_far,
        border_tiles,
        t_par,
    )
    chosen, line = earlier_rows(earlier_panels, used_panels)
    part, line = lax.optimization_barrier((part, line))
    spread = lax.all_to_all(part.reshape(4096, SLAB_W), CHIPS, 0, 0, tiled=True)
    total = spread.reshape(64, 2, 32, SLAB_W).astype(jnp.float32).sum(axis=0)
    held = jnp.where(c == 0, total[0], total[1])
    got = moved(jnp.where(c == 0, total[1], total[0]), dc=1)
    coupling = jnp.concatenate(
        [jnp.where(c == 0, held, got), jnp.where(c == 0, got, held)], axis=1
    )
    earlier = earlier_term(chosen, line)
    return base_slab - coupling - earlier


def solution(mesh):
    split = jax.sharding.Mesh(mesh.devices.reshape(4, 2, 2, 4, 2), AXES)
    scen, intr = ("y", "xl"), ("xh", "z", "c")
    return jax.shard_map(
        on_device,
        mesh=split,
        in_specs=(
            P(scen, intr, None),
            P(scen, intr, None),
            P(scen, None, intr, None),
            P(scen, None),
            P(scen, None),
            P(scen),
            P(AXES, None),
            P(None, AXES, None),
            P(),
        ),
        out_specs=P(AXES, None),
        check_vma=False,
    )
```

```python
import functools

import jax
import jax.numpy as jnp
from jax import lax
from jax.experimental import pallas as pl
from jax.experimental.pallas import tpu as pltpu
from jax.sharding import PartitionSpec as P


COLS = 512
SLAB_W = 256
TILE = 128
LIST = 16
NTILE = 32
HERE = 4
ROWS_HERE = 256
CHIP_ROWS = 512
BATCH = 2
AXES = ("y", "xl", "xh", "z", "c")
CHIPS = ("y", "xl", "xh", "z")


def device_at(x, y, z, c):
    return (((y * 2 + x % 2) * 2 + x // 2) * 4 + z) * 2 + c


def everyone():
    return [(x, y, z, c) for x in range(4) for y in range(4) for z in range(4) for c in range(2)]


def moved(array, dx=0, dy=0, dz=0, dc=0):
    pairs = [
        (device_at(x, y, z, c), device_at((x + dx) % 4, (y + dy) % 4, (z + dz) % 4, (c + dc) % 2))
        for x, y, z, c in everyone()
    ]
    return lax.ppermute(array, AXES, sorted(pairs))


ANY = pl.BlockSpec(memory_space=pl.ANY)
SCALAR = pl.BlockSpec(memory_space=pltpu.SMEM)


def layout(groups):
    operands, plan = [], []
    for s, group in enumerate(groups):
        for array, block, where in group:
            at = next((i for i, operand in enumerate(operands) if operand is array), len(operands))
            if at == len(operands):
                operands.append(array)
            plan.append((s, at, block, where))
    return operands, plan


def fetches(plan, place, blocks, inv_own, inv_par, held, turned, sems):
    units = []
    for n, (s, at, block, (far, shift)) in enumerate(plan):
        chip = lax.rem(place[0] + far, 2) * 4 + lax.rem(place[1] + shift, 4)
        columns = pl.ds(pl.multiple_of(chip * CHIP_ROWS, CHIP_ROWS), CHIP_ROWS)
        upper, lower = pl.ds(0, ROWS_HERE), pl.ds(ROWS_HERE, ROWS_HERE)
        units.append(
            [
                pltpu.make_async_copy(blocks[at].at[block], held.at[n], sems.at[n]),
                pltpu.make_async_copy(inv_own.at[s, :, columns], turned.at[n, upper], sems.at[n]),
                pltpu.make_async_copy(inv_par.at[s, :, columns], turned.at[n, lower], sems.at[n]),
            ]
        )
    return units


def added(s, plan, units, held, turned):
    total = None
    for n, unit in enumerate(plan):
        if unit[0] == s:
            for copy in units[n]:
                copy.wait()
            term = jnp.dot(turned[n], held[n], preferred_element_type=jnp.float32)
            total = term if total is None else total + term
    return total


def stage_body(plan, count, has_sum, place, *refs):
    blocks, (inv_own, inv_par, *refs) = refs[:count], refs[count:]
    so_far, refs = (refs[0], refs[1:]) if has_sum else (None, refs)
    out, held, turned, kept, unit_sems, sum_sems, out_sems = refs
    units = fetches(plan, place, blocks, inv_own, inv_par, held, turned, unit_sems)
    sums = []
    if has_sum:
        sums = [
            pltpu.make_async_copy(so_far.at[s], kept.at[s], sum_sems.at[s]) for s in range(HERE)
        ]
    for s in range(HERE):
        for n, unit in enumerate(plan):
            if unit[0] == s:
                for copy in units[n]:
                    copy.start()
        if has_sum:
            sums[s].start()
    writes = []
    for s in range(HERE):
        total = added(s, plan, units, held, turned)
        if has_sum:
            sums[s].wait()
            total = total + kept[s]
        kept[s] = total
        write = pltpu.make_async_copy(kept.at[s], out.at[s], out_sems.at[s])
        write.start()
        writes.append(write)
    for write in writes:
        write.wait()


def stage(place, inv_own, inv_par, groups, so_far=None):
    operands, plan = layout(groups)
    units = len(plan)
    has_sum = so_far is not None
    return pl.pallas_call(
        functools.partial(stage_body, plan, len(operands), has_sum),
        out_shape=jax.ShapeDtypeStruct((HERE, CHIP_ROWS, SLAB_W), jnp.float32),
        in_specs=[SCALAR] + [ANY] * (len(operands) + 2 + has_sum),
        out_specs=ANY,
        scratch_shapes=[
            pltpu.VMEM((units, CHIP_ROWS, SLAB_W), jnp.bfloat16),
            pltpu.VMEM((units, CHIP_ROWS, CHIP_ROWS), jnp.bfloat16),
            pltpu.VMEM((HERE, CHIP_ROWS, SLAB_W), jnp.float32),
            pltpu.SemaphoreType.DMA((units,)),
            pltpu.SemaphoreType.DMA((HERE,)),
            pltpu.SemaphoreType.DMA((HERE,)),
        ],
        cost_estimate=pl.CostEstimate(
            flops=units * 2 * 512 * 512 * 256, bytes_accessed=units << 19, transcendentals=0
        ),
    )(place, *operands, inv_own, inv_par, *([so_far] if has_sum else []))


def couple_body(plan, count, place, rows, slabs, counts, *refs):
    blocks, refs = refs[:count], refs[count:]
    inv_own, inv_par, so_far, t_own, t_par, out, held, turned, kept, tiles, acc, rounded = refs[:12]
    applied, found_rows, found_count, unit_sems, sum_sems, tile_sems, out_sems = refs[12:]
    units = fetches(plan, place, blocks, inv_own, inv_par, held, turned, unit_sems)
    sums = [pltpu.make_async_copy(so_far.at[s], kept.at[s], sum_sems.at[s]) for s in range(HERE)]

    def tile_copies(s, l, slot):
        upper, lower = pl.ds(0, ROWS_HERE), pl.ds(ROWS_HERE, ROWS_HERE)
        return (
            pltpu.make_async_copy(t_own.at[s, l], tiles.at[s, slot, upper], tile_sems.at[s]),
            pltpu.make_async_copy(t_par.at[s, l], tiles.at[s, slot, lower], tile_sems.at[s]),
        )

    for s in range(HERE):
        for n, unit in enumerate(plan):
            if unit[0] == s:
                for copy in units[n]:
                    copy.start()
        sums[s].start()

        def look(l, found, s=s):
            hit = slabs[s, l] == place[2]

            @pl.when(hit)
            def _():
                found_rows[s, found] = rows[s, l]
                for copy in tile_copies(s, l, found):
                    copy.start()

            return found + hit.astype(jnp.int32)

        found_count[s] = lax.fori_loop(0, counts[s], look, jnp.int32(0))
    acc[...] = jnp.zeros_like(acc)
    for s in range(HERE):
        total = added(s, plan, units, held, turned)
        sums[s].wait()
        applied[...] = (total + kept[s]).astype(jnp.bfloat16)
        found = found_count[s]

        def landed(slot, carry, s=s):
            for copy in tile_copies(s, 0, slot):
                copy.wait()
            return carry

        lax.fori_loop(0, found, landed, 0)

        def step(b, carry, s=s, found=found):
            left = jnp.concatenate([tiles[s, b * BATCH + j].T for j in range(BATCH)], axis=0)
            term = jnp.dot(left, applied[...], preferred_element_type=jnp.float32)
            for j in range(BATCH):

                @pl.when(b * BATCH + j < found)
                def _():
                    acc[found_rows[s, b * BATCH + j]] += term[j * TILE : (j + 1) * TILE]

            return carry

        lax.fori_loop(0, (found + BATCH - 1) // BATCH, step, 0)
    writes = []
    for part in range(4):
        span = pl.ds(part * (NTILE // 4), NTILE // 4)
        rounded[span] = acc[span].astype(jnp.bfloat16)
        write = pltpu.make_async_copy(rounded.at[span], out.at[span], out_sems.at[part])
        write.start()
        writes.append(write)
    for write in writes:
        write.wait()


def couple(place, rows, slabs, counts, inv_own, inv_par, groups, so_far, t_own, t_par):
    operands, plan = layout(groups)
    units = len(plan)
    return pl.pallas_call(
        functools.partial(couple_body, plan, len(operands)),
        out_shape=jax.ShapeDtypeStruct((NTILE, TILE, SLAB_W), jnp.bfloat16),
        in_specs=[SCALAR] * 4 + [ANY] * (len(operands) + 5),
        out_specs=ANY,
        scratch_shapes=[
            pltpu.VMEM((units, CHIP_ROWS, SLAB_W), jnp.bfloat16),
            pltpu.VMEM((units, CHIP_ROWS, CHIP_ROWS), jnp.bfloat16),
            pltpu.VMEM((HERE, CHIP_ROWS, SLAB_W), jnp.float32),
            pltpu.VMEM((HERE, LIST, CHIP_ROWS, TILE), jnp.bfloat16),
            pltpu.VMEM((NTILE, TILE, SLAB_W), jnp.float32),
            pltpu.VMEM((NTILE, TILE, SLAB_W), jnp.bfloat16),
            pltpu.VMEM((CHIP_ROWS, SLAB_W), jnp.bfloat16),
            pltpu.SMEM((HERE, LIST), jnp.int32),
            pltpu.SMEM((HERE,), jnp.int32),
            pltpu.SemaphoreType.DMA((units,)),
            pltpu.SemaphoreType.DMA((HERE,)),
            pltpu.SemaphoreType.DMA((HERE,)),
            pltpu.SemaphoreType.DMA((4,)),
        ],
        cost_estimate=pl.CostEstimate(flops=3 << 30, bytes_accessed=12 << 20, transcendentals=0),
        name="couple",
    )(
        place,
        rows,
        slabs,
        counts,
        *operands,
        inv_own,
        inv_par,
        so_far,
        t_own,
        t_par,
    )


def to_all(array, axes, size):
    return lax.all_to_all(
        jnp.broadcast_to(array[None], (size, *array.shape)), axes, 0, 0, tiled=True
    )


def earlier_rows(earlier_panels, used_panels):
    chosen = earlier_panels[used_panels]
    top = to_all(chosen, ("y", "xl"), 8)[0]
    return chosen, to_all(top, ("xh", "z", "c"), 16)


def earlier_term(chosen, line):
    top_rows = line.transpose(1, 0, 2, 3).reshape(4, COLS, TILE)
    return jnp.einsum("prt,pct->rc", chosen, top_rows, preferred_element_type=jnp.float32)


def on_device(
    inverse_panels,
    border_columns,
    border_tiles,
    tile_rows,
    tile_slabs,
    tile_count,
    base_slab,
    earlier_panels,
    used_panels,
):
    xh = lax.axis_index("xh")
    z = lax.axis_index("z")
    c = lax.axis_index("c")
    place = jnp.stack([xh, z, c]).astype(jnp.int32)

    low, high = border_columns[:, :, :SLAB_W], border_columns[:, :, SLAB_W:]
    got = moved(jnp.where(c == 0, high, low), dc=1)
    mine = jnp.where(
        c == 0, jnp.concatenate([low, got], axis=1), jnp.concatenate([got, high], axis=1)
    )
    inv_par = moved(inverse_panels, dc=1)
    t_par = moved(border_tiles, dc=1)

    a0, b0 = mine[:2], mine[2:]
    bx = moved(b0, dx=2)
    ap = moved(a0, dz=-1)
    am = moved(a0, dz=1)
    xa0 = moved(a0, dx=2)
    bb = jnp.concatenate([b0, bx], axis=0)
    bp = moved(bb, dz=-1)
    bm = moved(bb, dz=1)
    a2 = moved(am, dz=1)
    xa1 = moved(jnp.concatenate([am, ap], axis=0), dx=2)
    xa2 = moved(a2, dx=2)
    b2a = moved(bp[:3], dz=-1)
    b2b = moved(bm[3:], dz=1)

    near, far = 0, 1
    so_far = stage(
        place,
        inverse_panels,
        inv_par,
        [
            [
                (a0, g, (near, 0)),
                (am, g, (near, 3)),
                (ap, g, (near, 1)),
                (a2, g, (near, 2)),
                (xa0, g, (far, 0)),
            ]
            for g in range(2)
        ]
        + [
            [
                (bb, g, (near, 0)),
                (bb, 2 + g, (far, 0)),
                (bp, g, (near, 1)),
                (bp, 2 + g, (far, 1)),
            ]
            for g in range(2)
        ],
    )
    so_far = stage(
        place,
        inverse_panels,
        inv_par,
        [[(xa1, g, (far, 3)), (xa1, 2 + g, (far, 1))] for g in range(2)]
        + [[(bm, g, (near, 3)), (bm, 2 + g, (far, 3))] for g in range(2)],
        so_far,
    )
    part = couple(
        place,
        tile_rows,
        tile_slabs,
        tile_count,
        inverse_panels,
        inv_par,
        [
            [(xa2, 0, (far, 2))],
            [(xa2, 1, (far, 2))],
            [(b2a, 0, (near, 2)), (b2a, 2, (far, 2))],
            [(b2a, 1, (near, 2)), (b2b, 0, (far, 2))],
        ],
        so_far,
        border_tiles,
        t_par,
    )
    chosen, line = earlier_rows(earlier_panels, used_panels)
    part, line = lax.optimization_barrier((part, line))
    spread = lax.all_to_all(part.reshape(4096, SLAB_W), CHIPS, 0, 0, tiled=True)
    total = spread.reshape(64, 2, 32, SLAB_W).astype(jnp.float32).sum(axis=0)
    held = jnp.where(c == 0, total[0], total[1])
    got = moved(jnp.where(c == 0, total[1], total[0]), dc=1)
    coupling = jnp.concatenate(
        [jnp.where(c == 0, held, got), jnp.where(c == 0, got, held)], axis=1
    )
    earlier = earlier_term(chosen, line)
    return base_slab - coupling - earlier


def solution(mesh):
    split = jax.sharding.Mesh(mesh.devices.reshape(4, 2, 2, 4, 2), AXES)
    scen, intr = ("y", "xl"), ("xh", "z", "c")
    return jax.shard_map(
        on_device,
        mesh=split,
        in_specs=(
            P(scen, intr, None),
            P(scen, intr, None),
            P(scen, None, intr, None),
            P(scen, None),
            P(scen, None),
            P(scen),
            P(AXES, None),
            P(None, AXES, None),
            P(),
        ),
        out_specs=P(AXES, None),
        check_vma=False,
    )
```

```python
import functools

import jax
import jax.numpy as jnp
from jax import lax
from jax.experimental import pallas as pl
from jax.experimental.pallas import tpu as pltpu
from jax.sharding import PartitionSpec as P


COLS = 512
SLAB_W = 256
TILE = 128
LIST = 16
NTILE = 32
HERE = 4
ROWS_HERE = 256
CHIP_ROWS = 512
BATCH = 2
AXES = ("y", "xl", "xh", "z", "c")
CHIPS = ("y", "xl", "xh", "z")


def device_at(x, y, z, c):
    return (((y * 2 + x % 2) * 2 + x // 2) * 4 + z) * 2 + c


def everyone():
    return [(x, y, z, c) for x in range(4) for y in range(4) for z in range(4) for c in range(2)]


def moved(array, dx=0, dy=0, dz=0, dc=0):
    pairs = [
        (device_at(x, y, z, c), device_at((x + dx) % 4, (y + dy) % 4, (z + dz) % 4, (c + dc) % 2))
        for x, y, z, c in everyone()
    ]
    return lax.ppermute(array, AXES, sorted(pairs))


ANY = pl.BlockSpec(memory_space=pl.ANY)
SCALAR = pl.BlockSpec(memory_space=pltpu.SMEM)


def layout(groups):
    operands, plan = [], []
    for s, group in enumerate(groups):
        for array, block, where in group:
            at = next((i for i, operand in enumerate(operands) if operand is array), len(operands))
            if at == len(operands):
                operands.append(array)
            plan.append((s, at, block, where))
    return operands, plan


def fetches(plan, place, blocks, inv_own, inv_par, held, turned, sems):
    units = []
    for n, (s, at, block, (far, shift)) in enumerate(plan):
        chip = lax.rem(place[0] + far, 2) * 4 + lax.rem(place[1] + shift, 4)
        columns = pl.ds(pl.multiple_of(chip * CHIP_ROWS, CHIP_ROWS), CHIP_ROWS)
        upper, lower = pl.ds(0, ROWS_HERE), pl.ds(ROWS_HERE, ROWS_HERE)
        units.append(
            [
                pltpu.make_async_copy(blocks[at].at[block], held.at[n], sems.at[n]),
                pltpu.make_async_copy(inv_own.at[s, :, columns], turned.at[n, upper], sems.at[n]),
                pltpu.make_async_copy(inv_par.at[s, :, columns], turned.at[n, lower], sems.at[n]),
            ]
        )
    return units


def added(s, plan, units, held, turned):
    total = None
    for n, unit in enumerate(plan):
        if unit[0] == s:
            for copy in units[n]:
                copy.wait()
            term = jnp.dot(turned[n], held[n], preferred_element_type=jnp.float32)
            total = term if total is None else total + term
    return total


def stage_body(plan, count, has_sum, place, *refs):
    blocks, (inv_own, inv_par, *refs) = refs[:count], refs[count:]
    so_far, refs = (refs[0], refs[1:]) if has_sum else (None, refs)
    out, held, turned, kept, unit_sems, sum_sems, out_sems = refs
    units = fetches(plan, place, blocks, inv_own, inv_par, held, turned, unit_sems)
    sums = []
    if has_sum:
        sums = [
            pltpu.make_async_copy(so_far.at[s], kept.at[s], sum_sems.at[s]) for s in range(HERE)
        ]
    for s in range(HERE):
        for n, unit in enumerate(plan):
            if unit[0] == s:
                for copy in units[n]:
                    copy.start()
        if has_sum:
            sums[s].start()
    writes = []
    for s in range(HERE):
        total = added(s, plan, units, held, turned)
        if has_sum:
            sums[s].wait()
            total = total + kept[s]
        kept[s] = total
        write = pltpu.make_async_copy(kept.at[s], out.at[s], out_sems.at[s])
        write.start()
        writes.append(write)
    for write in writes:
        write.wait()


def stage(place, inv_own, inv_par, groups, so_far=None):
    operands, plan = layout(groups)
    units = len(plan)
    has_sum = so_far is not None
    return pl.pallas_call(
        functools.partial(stage_body, plan, len(operands), has_sum),
        out_shape=jax.ShapeDtypeStruct((HERE, CHIP_ROWS, SLAB_W), jnp.float32),
        in_specs=[SCALAR] + [ANY] * (len(operands) + 2 + has_sum),
        out_specs=ANY,
        scratch_shapes=[
            pltpu.VMEM((units, CHIP_ROWS, SLAB_W), jnp.bfloat16),
            pltpu.VMEM((units, CHIP_ROWS, CHIP_ROWS), jnp.bfloat16),
            pltpu.VMEM((HERE, CHIP_ROWS, SLAB_W), jnp.float32),
            pltpu.SemaphoreType.DMA((units,)),
            pltpu.SemaphoreType.DMA((HERE,)),
            pltpu.SemaphoreType.DMA((HERE,)),
        ],
        cost_estimate=pl.CostEstimate(
            flops=units * 2 * 512 * 512 * 256, bytes_accessed=units << 19, transcendentals=0
        ),
    )(place, *operands, inv_own, inv_par, *([so_far] if has_sum else []))


def couple_body(plan, count, place, rows, slabs, counts, *refs):
    blocks, refs = refs[:count], refs[count:]
    inv_own, inv_par, so_far, t_own, t_par, out, held, turned, kept, tiles, acc, rounded = refs[:12]
    applied, found_rows, found_count, unit_sems, sum_sems, tile_sems, out_sems = refs[12:]
    units = fetches(plan, place, blocks, inv_own, inv_par, held, turned, unit_sems)
    sums = [pltpu.make_async_copy(so_far.at[s], kept.at[s], sum_sems.at[s]) for s in range(HERE)]

    def tile_copies(s, l, slot):
        upper, lower = pl.ds(0, ROWS_HERE), pl.ds(ROWS_HERE, ROWS_HERE)
        return (
            pltpu.make_async_copy(t_own.at[s, l], tiles.at[s, slot, upper], tile_sems.at[s]),
            pltpu.make_async_copy(t_par.at[s, l], tiles.at[s, slot, lower], tile_sems.at[s]),
        )

    for s in range(HERE):
        for n, unit in enumerate(plan):
            if unit[0] == s:
                for copy in units[n]:
                    copy.start()
        sums[s].start()

        def look(l, found, s=s):
            hit = slabs[s, l] == place[2]

            @pl.when(hit)
            def _():
                found_rows[s, found] = rows[s, l]
                for copy in tile_copies(s, l, found):
                    copy.start()

            return found + hit.astype(jnp.int32)

        found_count[s] = lax.fori_loop(0, counts[s], look, jnp.int32(0))
    acc[...] = jnp.zeros_like(acc)
    for s in range(HERE):
        total = added(s, plan, units, held, turned)
        sums[s].wait()
        applied[...] = (total + kept[s]).astype(jnp.bfloat16)
        found = found_count[s]

        def landed(slot, carry, s=s):
            for copy in tile_copies(s, 0, slot):
                copy.wait()
            return carry

        lax.fori_loop(0, found, landed, 0)

        def step(b, carry, s=s, found=found):
            left = jnp.concatenate([tiles[s, b * BATCH + j].T for j in range(BATCH)], axis=0)
            term = jnp.dot(left, applied[...], preferred_element_type=jnp.float32)
            for j in range(BATCH):

                @pl.when(b * BATCH + j < found)
                def _():
                    acc[found_rows[s, b * BATCH + j]] += term[j * TILE : (j + 1) * TILE]

            return carry

        lax.fori_loop(0, (found + BATCH - 1) // BATCH, step, 0)
    writes = []
    for part in range(4):
        span = pl.ds(part * (NTILE // 4), NTILE // 4)
        rounded[span] = acc[span].astype(jnp.bfloat16)
        write = pltpu.make_async_copy(rounded.at[span], out.at[span], out_sems.at[part])
        write.start()
        writes.append(write)
    for write in writes:
        write.wait()


def couple(place, rows, slabs, counts, inv_own, inv_par, groups, so_far, t_own, t_par):
    operands, plan = layout(groups)
    units = len(plan)
    return pl.pallas_call(
        functools.partial(couple_body, plan, len(operands)),
        out_shape=jax.ShapeDtypeStruct((NTILE, TILE, SLAB_W), jnp.bfloat16),
        in_specs=[SCALAR] * 4 + [ANY] * (len(operands) + 5),
        out_specs=ANY,
        scratch_shapes=[
            pltpu.VMEM((units, CHIP_ROWS, SLAB_W), jnp.bfloat16),
            pltpu.VMEM((units, CHIP_ROWS, CHIP_ROWS), jnp.bfloat16),
            pltpu.VMEM((HERE, CHIP_ROWS, SLAB_W), jnp.float32),
            pltpu.VMEM((HERE, LIST, CHIP_ROWS, TILE), jnp.bfloat16),
            pltpu.VMEM((NTILE, TILE, SLAB_W), jnp.float32),
            pltpu.VMEM((NTILE, TILE, SLAB_W), jnp.bfloat16),
            pltpu.VMEM((CHIP_ROWS, SLAB_W), jnp.bfloat16),
            pltpu.SMEM((HERE, LIST), jnp.int32),
            pltpu.SMEM((HERE,), jnp.int32),
            pltpu.SemaphoreType.DMA((units,)),
            pltpu.SemaphoreType.DMA((HERE,)),
            pltpu.SemaphoreType.DMA((HERE,)),
            pltpu.SemaphoreType.DMA((4,)),
        ],
        cost_estimate=pl.CostEstimate(flops=3 << 30, bytes_accessed=12 << 20, transcendentals=0),
        name="couple",
    )(
        place,
        rows,
        slabs,
        counts,
        *operands,
        inv_own,
        inv_par,
        so_far,
        t_own,
        t_par,
    )


def to_all(array, axes, size):
    return lax.all_to_all(
        jnp.broadcast_to(array[None], (size, *array.shape)), axes, 0, 0, tiled=True
    )


def earlier_term(earlier_panels, used_panels, xh, z, c):
    chosen = earlier_panels[used_panels]
    top = to_all(chosen, ("y", "xl"), 8)[0]
    prev = moved(top, dz=1)
    after = moved(top, dz=-1)
    line = jnp.stack([top, after, moved(top, dz=2), prev])
    plane = jnp.concatenate([line, moved(line, dx=2)], axis=0)
    both = jnp.concatenate([plane, moved(plane, dc=1)], axis=0)
    intr = jnp.arange(16, dtype=jnp.int32)
    far = lax.rem(intr // 8 + xh, 2)
    shift = lax.rem(intr // 2 % 4 + 4 - z, 4)
    other = lax.rem(intr % 2 + c, 2)
    ordered = both[other * 8 + far * 4 + shift]
    top_rows = ordered.transpose(1, 0, 2, 3).reshape(4, COLS, TILE)
    product = jnp.einsum("prt,pct->rc", chosen, top_rows, preferred_element_type=jnp.float32)
    return lax.optimization_barrier(product)


def on_device(
    inverse_panels,
    border_columns,
    border_tiles,
    tile_rows,
    tile_slabs,
    tile_count,
    base_slab,
    earlier_panels,
    used_panels,
):
    xh = lax.axis_index("xh")
    z = lax.axis_index("z")
    c = lax.axis_index("c")
    place = jnp.stack([xh, z, c]).astype(jnp.int32)

    low, high = border_columns[:, :, :SLAB_W], border_columns[:, :, SLAB_W:]
    got = moved(jnp.where(c == 0, high, low), dc=1)
    mine = jnp.where(
        c == 0, jnp.concatenate([low, got], axis=1), jnp.concatenate([got, high], axis=1)
    )
    inv_par = moved(inverse_panels, dc=1)
    t_par = moved(border_tiles, dc=1)

    a0, b0 = mine[:2], mine[2:]
    bx = moved(b0, dx=2)
    ap = moved(a0, dz=-1)
    am = moved(a0, dz=1)
    xa0 = moved(a0, dx=2)
    bb = jnp.concatenate([b0, bx], axis=0)
    bp = moved(bb, dz=-1)
    bm = moved(bb, dz=1)
    a2 = moved(am, dz=1)
    xa1 = moved(jnp.concatenate([am, ap], axis=0), dx=2)
    xa2 = moved(a2, dx=2)
    b2a = moved(bp[:3], dz=-1)
    b2b = moved(bm[3:], dz=1)

    near, far = 0, 1
    so_far = stage(
        place,
        inverse_panels,
        inv_par,
        [
            [
                (a0, g, (near, 0)),
                (am, g, (near, 3)),
                (ap, g, (near, 1)),
                (a2, g, (near, 2)),
                (xa0, g, (far, 0)),
            ]
            for g in range(2)
        ]
        + [
            [
                (bb, g, (near, 0)),
                (bb, 2 + g, (far, 0)),
            ]
            for g in range(2)
        ],
    )
    so_far = stage(
        place,
        inverse_panels,
        inv_par,
        [[(xa1, g, (far, 3)), (xa1, 2 + g, (far, 1))] for g in range(2)]
        + [
            [
                (bp, g, (near, 1)),
                (bp, 2 + g, (far, 1)),
                (bm, g, (near, 3)),
                (bm, 2 + g, (far, 3)),
            ]
            for g in range(2)
        ],
        so_far,
    )
    part = couple(
        place,
        tile_rows,
        tile_slabs,
        tile_count,
        inverse_panels,
        inv_par,
        [
            [(xa2, 0, (far, 2))],
            [(xa2, 1, (far, 2))],
            [(b2a, 0, (near, 2)), (b2a, 2, (far, 2))],
            [(b2a, 1, (near, 2)), (b2b, 0, (far, 2))],
        ],
        so_far,
        border_tiles,
        t_par,
    )
    earlier = earlier_term(earlier_panels, used_panels, xh, z, c)
    spread = lax.all_to_all(part.reshape(4096, SLAB_W), CHIPS, 0, 0, tiled=True)
    total = spread.reshape(64, 2, 32, SLAB_W).astype(jnp.float32).sum(axis=0)
    held = jnp.where(c == 0, total[0], total[1])
    got = moved(jnp.where(c == 0, total[1], total[0]), dc=1)
    coupling = jnp.concatenate(
        [jnp.where(c == 0, held, got), jnp.where(c == 0, got, held)], axis=1
    )
    return base_slab - coupling - earlier


def solution(mesh):
    split = jax.sharding.Mesh(mesh.devices.reshape(4, 2, 2, 4, 2), AXES)
    scen, intr = ("y", "xl"), ("xh", "z", "c")
    return jax.shard_map(
        on_device,
        mesh=split,
        in_specs=(
            P(scen, intr, None),
            P(scen, intr, None),
            P(scen, None, intr, None),
            P(scen, None),
            P(scen, None),
            P(scen),
            P(AXES, None),
            P(None, AXES, None),
            P(),
        ),
        out_specs=P(AXES, None),
        check_vma=False,
    )
```

```python
import functools

import jax
import jax.numpy as jnp
from jax import lax
from jax.experimental import pallas as pl
from jax.experimental.pallas import tpu as pltpu
from jax.sharding import PartitionSpec as P


COLS = 512
SLAB_W = 256
TILE = 128
LIST = 16
NTILE = 32
HERE = 4
ROWS_HERE = 256
CHIP_ROWS = 512
BATCH = 2
AXES = ("y", "xl", "xh", "z", "c")
CHIPS = ("y", "xl", "xh", "z")


def device_at(x, y, z, c):
    return (((y * 2 + x % 2) * 2 + x // 2) * 4 + z) * 2 + c


def everyone():
    return [(x, y, z, c) for x in range(4) for y in range(4) for z in range(4) for c in range(2)]


def moved(array, dx=0, dy=0, dz=0, dc=0):
    pairs = [
        (device_at(x, y, z, c), device_at((x + dx) % 4, (y + dy) % 4, (z + dz) % 4, (c + dc) % 2))
        for x, y, z, c in everyone()
    ]
    return lax.ppermute(array, AXES, sorted(pairs))


ANY = pl.BlockSpec(memory_space=pl.ANY)
SCALAR = pl.BlockSpec(memory_space=pltpu.SMEM)


def layout(groups):
    operands, plan = [], []
    for s, group in enumerate(groups):
        for array, block, where in group:
            at = next((i for i, operand in enumerate(operands) if operand is array), len(operands))
            if at == len(operands):
                operands.append(array)
            plan.append((s, at, block, where))
    return operands, plan


def fetches(plan, place, blocks, inv_own, inv_par, held, turned, sems):
    units = []
    for n, (s, at, block, (far, shift)) in enumerate(plan):
        chip = lax.rem(place[0] + far, 2) * 4 + lax.rem(place[1] + shift, 4)
        columns = pl.ds(pl.multiple_of(chip * CHIP_ROWS, CHIP_ROWS), CHIP_ROWS)
        upper, lower = pl.ds(0, ROWS_HERE), pl.ds(ROWS_HERE, ROWS_HERE)
        units.append(
            [
                pltpu.make_async_copy(blocks[at].at[block], held.at[n], sems.at[n]),
                pltpu.make_async_copy(inv_own.at[s, :, columns], turned.at[n, upper], sems.at[n]),
                pltpu.make_async_copy(inv_par.at[s, :, columns], turned.at[n, lower], sems.at[n]),
            ]
        )
    return units


def added(s, plan, units, held, turned):
    total = None
    for n, unit in enumerate(plan):
        if unit[0] == s:
            for copy in units[n]:
                copy.wait()
            term = jnp.dot(turned[n], held[n], preferred_element_type=jnp.float32)
            total = term if total is None else total + term
    return total


def stage_body(plan, count, has_sum, place, *refs):
    blocks, (inv_own, inv_par, *refs) = refs[:count], refs[count:]
    so_far, refs = (refs[0], refs[1:]) if has_sum else (None, refs)
    out, held, turned, kept, unit_sems, sum_sems, out_sems = refs
    units = fetches(plan, place, blocks, inv_own, inv_par, held, turned, unit_sems)
    touched = sorted({unit[0] for unit in plan})
    sums = {}
    for s in touched:
        for n, unit in enumerate(plan):
            if unit[0] == s:
                for copy in units[n]:
                    copy.start()
        if has_sum:
            sums[s] = pltpu.make_async_copy(so_far.at[s], kept.at[s], sum_sems.at[s])
            sums[s].start()
    writes = []
    for s in touched:
        total = added(s, plan, units, held, turned)
        if has_sum:
            sums[s].wait()
            total = total + kept[s]
        kept[s] = total
        write = pltpu.make_async_copy(kept.at[s], out.at[s], out_sems.at[s])
        write.start()
        writes.append(write)
    for write in writes:
        write.wait()


def stage(place, inv_own, inv_par, groups, so_far=None):
    operands, plan = layout(groups)
    units = len(plan)
    has_sum = so_far is not None
    return pl.pallas_call(
        functools.partial(stage_body, plan, len(operands), has_sum),
        out_shape=jax.ShapeDtypeStruct((HERE, CHIP_ROWS, SLAB_W), jnp.float32),
        in_specs=[SCALAR] + [ANY] * (len(operands) + 2 + has_sum),
        out_specs=ANY,
        scratch_shapes=[
            pltpu.VMEM((units, CHIP_ROWS, SLAB_W), jnp.bfloat16),
            pltpu.VMEM((units, CHIP_ROWS, CHIP_ROWS), jnp.bfloat16),
            pltpu.VMEM((HERE, CHIP_ROWS, SLAB_W), jnp.float32),
            pltpu.SemaphoreType.DMA((units,)),
            pltpu.SemaphoreType.DMA((HERE,)),
            pltpu.SemaphoreType.DMA((HERE,)),
        ],
        cost_estimate=pl.CostEstimate(
            flops=units * 2 * 512 * 512 * 256, bytes_accessed=units << 19, transcendentals=0
        ),
        input_output_aliases={len(operands) + 3: 0} if has_sum else {},
    )(place, *operands, inv_own, inv_par, *([so_far] if has_sum else []))


def couple_body(plan, count, place, rows, slabs, counts, *refs):
    blocks, refs = refs[:count], refs[count:]
    inv_own, inv_par, so_far, t_own, t_par, out, held, turned, kept, tiles, acc, rounded = refs[:12]
    applied, found_rows, found_count, unit_sems, sum_sems, tile_sems, out_sems = refs[12:]
    units = fetches(plan, place, blocks, inv_own, inv_par, held, turned, unit_sems)
    sums = [pltpu.make_async_copy(so_far.at[s], kept.at[s], sum_sems.at[s]) for s in range(HERE)]

    def tile_copies(s, l, slot):
        upper, lower = pl.ds(0, ROWS_HERE), pl.ds(ROWS_HERE, ROWS_HERE)
        return (
            pltpu.make_async_copy(t_own.at[s, l], tiles.at[s, slot, upper], tile_sems.at[s]),
            pltpu.make_async_copy(t_par.at[s, l], tiles.at[s, slot, lower], tile_sems.at[s]),
        )

    for s in range(HERE):
        for n, unit in enumerate(plan):
            if unit[0] == s:
                for copy in units[n]:
                    copy.start()
        sums[s].start()

        def look(l, found, s=s):
            hit = slabs[s, l] == place[2]

            @pl.when(hit)
            def _():
                found_rows[s, found] = rows[s, l]
                for copy in tile_copies(s, l, found):
                    copy.start()

            return found + hit.astype(jnp.int32)

        found_count[s] = lax.fori_loop(0, counts[s], look, jnp.int32(0))
    acc[...] = jnp.zeros_like(acc)
    for s in range(HERE):
        total = added(s, plan, units, held, turned)
        sums[s].wait()
        applied[...] = (total + kept[s]).astype(jnp.bfloat16)
        found = found_count[s]

        def landed(slot, carry, s=s):
            for copy in tile_copies(s, 0, slot):
                copy.wait()
            return carry

        lax.fori_loop(0, found, landed, 0)

        def step(b, carry, s=s, found=found):
            left = jnp.concatenate([tiles[s, b * BATCH + j].T for j in range(BATCH)], axis=0)
            term = jnp.dot(left, applied[...], preferred_element_type=jnp.float32)
            for j in range(BATCH):

                @pl.when(b * BATCH + j < found)
                def _():
                    acc[found_rows[s, b * BATCH + j]] += term[j * TILE : (j + 1) * TILE]

            return carry

        lax.fori_loop(0, (found + BATCH - 1) // BATCH, step, 0)
    writes = []
    for part in range(4):
        span = pl.ds(part * (NTILE // 4), NTILE // 4)
        rounded[span] = acc[span].astype(jnp.bfloat16)
        write = pltpu.make_async_copy(rounded.at[span], out.at[span], out_sems.at[part])
        write.start()
        writes.append(write)
    for write in writes:
        write.wait()


def couple(place, rows, slabs, counts, inv_own, inv_par, groups, so_far, t_own, t_par):
    operands, plan = layout(groups)
    units = len(plan)
    return pl.pallas_call(
        functools.partial(couple_body, plan, len(operands)),
        out_shape=jax.ShapeDtypeStruct((NTILE, TILE, SLAB_W), jnp.bfloat16),
        in_specs=[SCALAR] * 4 + [ANY] * (len(operands) + 5),
        out_specs=ANY,
        scratch_shapes=[
            pltpu.VMEM((units, CHIP_ROWS, SLAB_W), jnp.bfloat16),
            pltpu.VMEM((units, CHIP_ROWS, CHIP_ROWS), jnp.bfloat16),
            pltpu.VMEM((HERE, CHIP_ROWS, SLAB_W), jnp.float32),
            pltpu.VMEM((HERE, LIST, CHIP_ROWS, TILE), jnp.bfloat16),
            pltpu.VMEM((NTILE, TILE, SLAB_W), jnp.float32),
            pltpu.VMEM((NTILE, TILE, SLAB_W), jnp.bfloat16),
            pltpu.VMEM((CHIP_ROWS, SLAB_W), jnp.bfloat16),
            pltpu.SMEM((HERE, LIST), jnp.int32),
            pltpu.SMEM((HERE,), jnp.int32),
            pltpu.SemaphoreType.DMA((units,)),
            pltpu.SemaphoreType.DMA((HERE,)),
            pltpu.SemaphoreType.DMA((HERE,)),
            pltpu.SemaphoreType.DMA((4,)),
        ],
        cost_estimate=pl.CostEstimate(flops=3 << 30, bytes_accessed=12 << 20, transcendentals=0),
        name="couple",
    )(
        place,
        rows,
        slabs,
        counts,
        *operands,
        inv_own,
        inv_par,
        so_far,
        t_own,
        t_par,
    )


def to_all(array, axes, size):
    return lax.all_to_all(
        jnp.broadcast_to(array[None], (size, *array.shape)), axes, 0, 0, tiled=True
    )


def earlier_term(earlier_panels, used_panels, xh, z, c):
    chosen = earlier_panels[used_panels]
    top = to_all(chosen, ("y",), 4)[0]
    top = jnp.where(lax.axis_index("xl") == 1, moved(top, dx=1), top)
    prev = moved(top, dz=1)
    after = moved(top, dz=-1)
    opposite = moved(top, dz=2)
    line = jnp.stack([top, after, opposite, prev])
    plane = jnp.concatenate([line, moved(line, dx=2)], axis=0)
    both = jnp.concatenate([plane, moved(plane, dc=1)], axis=0)
    intr = jnp.arange(16, dtype=jnp.int32)
    far = lax.rem(intr // 8 + xh, 2)
    shift = lax.rem(intr // 2 % 4 + 4 - z, 4)
    other = lax.rem(intr % 2 + c, 2)
    ordered = both[other * 8 + far * 4 + shift]
    top_rows = ordered.transpose(1, 0, 2, 3).reshape(4, COLS, TILE)
    product = jnp.einsum("prt,pct->rc", chosen, top_rows, preferred_element_type=jnp.float32)
    return lax.optimization_barrier(product)


def on_device(
    inverse_panels,
    border_columns,
    border_tiles,
    tile_rows,
    tile_slabs,
    tile_count,
    base_slab,
    earlier_panels,
    used_panels,
):
    xh = lax.axis_index("xh")
    z = lax.axis_index("z")
    c = lax.axis_index("c")
    place = jnp.stack([xh, z, c]).astype(jnp.int32)

    low, high = border_columns[:, :, :SLAB_W], border_columns[:, :, SLAB_W:]
    got = moved(jnp.where(c == 0, high, low), dc=1)
    mine = jnp.where(
        c == 0, jnp.concatenate([low, got], axis=1), jnp.concatenate([got, high], axis=1)
    )
    inv_par = moved(inverse_panels, dc=1)
    t_par = moved(border_tiles, dc=1)

    a0, b0 = mine[:2], mine[2:]
    bx = moved(b0, dx=2)
    ap = moved(a0, dz=-1)
    am = moved(a0, dz=1)
    xa0 = moved(a0, dx=2)
    bb = jnp.concatenate([b0, bx], axis=0)
    bp = moved(bb, dz=-1)
    bm = moved(bb, dz=1)
    a2 = moved(am, dz=1)
    xa1 = moved(jnp.concatenate([am, ap], axis=0), dx=2)
    xa2 = moved(a2, dx=2)
    b2a = moved(bp[:3], dz=-1)
    b2b = moved(bm[3:], dz=1)

    near, far = 0, 1
    so_far = stage(
        place,
        inverse_panels,
        inv_par,
        [
            [
                (a0, g, (near, 0)),
                (am, g, (near, 3)),
                (ap, g, (near, 1)),
                (a2, g, (near, 2)),
                (xa0, g, (far, 0)),
            ]
            for g in range(2)
        ]
        + [
            [
                (bb, g, (near, 0)),
                (bb, 2 + g, (far, 0)),
            ]
            for g in range(2)
        ],
    )
    so_far = stage(
        place,
        inverse_panels,
        inv_par,
        [[(xa1, g, (far, 3)), (xa1, 2 + g, (far, 1))] for g in range(2)]
        + [[(bp, g, (near, 1)), (bp, 2 + g, (far, 1))] for g in range(2)],
        so_far,
    )
    so_far = stage(
        place,
        inverse_panels,
        inv_par,
        [[]] * 2 + [[(bm, g, (near, 3)), (bm, 2 + g, (far, 3))] for g in range(2)],
        so_far,
    )
    part = couple(
        place,
        tile_rows,
        tile_slabs,
        tile_count,
        inverse_panels,
        inv_par,
        [
            [(xa2, 0, (far, 2))],
            [(xa2, 1, (far, 2))],
            [(b2a, 0, (near, 2)), (b2a, 2, (far, 2))],
            [(b2a, 1, (near, 2)), (b2b, 0, (far, 2))],
        ],
        so_far,
        border_tiles,
        t_par,
    )
    earlier = earlier_term(earlier_panels, used_panels, xh, z, c)
    spread = lax.all_to_all(part.reshape(4096, SLAB_W), CHIPS, 0, 0, tiled=True)
    total = spread.reshape(64, 2, 32, SLAB_W).astype(jnp.float32).sum(axis=0)
    held = jnp.where(c == 0, total[0], total[1])
    got = moved(jnp.where(c == 0, total[1], total[0]), dc=1)
    coupling = jnp.concatenate(
        [jnp.where(c == 0, held, got), jnp.where(c == 0, got, held)], axis=1
    )
    return base_slab - coupling - earlier


def solution(mesh):
    split = jax.sharding.Mesh(mesh.devices.reshape(4, 2, 2, 4, 2), AXES)
    scen, intr = ("y", "xl"), ("xh", "z", "c")
    return jax.shard_map(
        on_device,
        mesh=split,
        in_specs=(
            P(scen, intr, None),
            P(scen, intr, None),
            P(scen, None, intr, None),
            P(scen, None),
            P(scen, None),
            P(scen),
            P(AXES, None),
            P(None, AXES, None),
            P(),
        ),
        out_specs=P(AXES, None),
        check_vma=False,
    )
```

```python
import functools

import jax
import jax.numpy as jnp
from jax import lax
from jax.experimental import pallas as pl
from jax.experimental.pallas import tpu as pltpu
from jax.sharding import PartitionSpec as P


COLS = 512
SLAB_W = 256
TILE = 128
LIST = 16
NTILE = 32
HERE = 4
ROWS_HERE = 256
CHIP_ROWS = 512
BATCH = 4
AXES = ("y", "xl", "xh", "z", "c")
CHIPS = ("y", "xl", "xh", "z")


def device_at(x, y, z, c):
    return (((y * 2 + x % 2) * 2 + x // 2) * 4 + z) * 2 + c


def everyone():
    return [(x, y, z, c) for x in range(4) for y in range(4) for z in range(4) for c in range(2)]


def moved(array, dx=0, dy=0, dz=0, dc=0):
    pairs = [
        (device_at(x, y, z, c), device_at((x + dx) % 4, (y + dy) % 4, (z + dz) % 4, (c + dc) % 2))
        for x, y, z, c in everyone()
    ]
    return lax.ppermute(array, AXES, sorted(pairs))


ANY = pl.BlockSpec(memory_space=pl.ANY)
SCALAR = pl.BlockSpec(memory_space=pltpu.SMEM)


def layout(groups):
    operands, plan = [], []
    for s, group in enumerate(groups):
        for array, block, where in group:
            at = next((i for i, operand in enumerate(operands) if operand is array), len(operands))
            if at == len(operands):
                operands.append(array)
            plan.append((s, at, block, where))
    return operands, plan


def fetches(plan, place, blocks, inv_own, inv_par, held, turned, sems):
    units = []
    for n, (s, at, block, (far, shift)) in enumerate(plan):
        chip = lax.rem(place[0] + far, 2) * 4 + lax.rem(place[1] + shift, 4)
        columns = pl.ds(pl.multiple_of(chip * CHIP_ROWS, CHIP_ROWS), CHIP_ROWS)
        upper, lower = pl.ds(0, ROWS_HERE), pl.ds(ROWS_HERE, ROWS_HERE)
        units.append(
            [
                pltpu.make_async_copy(blocks[at].at[block], held.at[n], sems.at[n]),
                pltpu.make_async_copy(inv_own.at[s, :, columns], turned.at[n, upper], sems.at[n]),
                pltpu.make_async_copy(inv_par.at[s, :, columns], turned.at[n, lower], sems.at[n]),
            ]
        )
    return units


def added(s, plan, units, held, turned):
    total = None
    for n, unit in enumerate(plan):
        if unit[0] == s:
            for copy in units[n]:
                copy.wait()
            term = jnp.dot(turned[n], held[n], preferred_element_type=jnp.float32)
            total = term if total is None else total + term
    return total


def stage_body(plan, count, has_sum, place, *refs):
    blocks, (inv_own, inv_par, *refs) = refs[:count], refs[count:]
    so_far, refs = (refs[0], refs[1:]) if has_sum else (None, refs)
    out, held, turned, kept, unit_sems, sum_sems, out_sems = refs
    units = fetches(plan, place, blocks, inv_own, inv_par, held, turned, unit_sems)
    touched = sorted({unit[0] for unit in plan})
    sums = {}
    for s in touched:
        for n, unit in enumerate(plan):
            if unit[0] == s:
                for copy in units[n]:
                    copy.start()
        if has_sum:
            sums[s] = pltpu.make_async_copy(so_far.at[s], kept.at[s], sum_sems.at[s])
            sums[s].start()
    writes = []
    for s in touched:
        total = added(s, plan, units, held, turned)
        if has_sum:
            sums[s].wait()
            total = total + kept[s]
        kept[s] = total
        write = pltpu.make_async_copy(kept.at[s], out.at[s], out_sems.at[s])
        write.start()
        writes.append(write)
    for write in writes:
        write.wait()


def stage(place, inv_own, inv_par, groups, so_far=None):
    operands, plan = layout(groups)
    units = len(plan)
    has_sum = so_far is not None
    return pl.pallas_call(
        functools.partial(stage_body, plan, len(operands), has_sum),
        out_shape=jax.ShapeDtypeStruct((HERE, CHIP_ROWS, SLAB_W), jnp.float32),
        in_specs=[SCALAR] + [ANY] * (len(operands) + 2 + has_sum),
        out_specs=ANY,
        scratch_shapes=[
            pltpu.VMEM((units, CHIP_ROWS, SLAB_W), jnp.bfloat16),
            pltpu.VMEM((units, CHIP_ROWS, CHIP_ROWS), jnp.bfloat16),
            pltpu.VMEM((HERE, CHIP_ROWS, SLAB_W), jnp.float32),
            pltpu.SemaphoreType.DMA((units,)),
            pltpu.SemaphoreType.DMA((HERE,)),
            pltpu.SemaphoreType.DMA((HERE,)),
        ],
        cost_estimate=pl.CostEstimate(
            flops=units * 2 * 512 * 512 * 256, bytes_accessed=units << 19, transcendentals=0
        ),
        input_output_aliases={len(operands) + 3: 0} if has_sum else {},
    )(place, *operands, inv_own, inv_par, *([so_far] if has_sum else []))


def couple_body(plan, count, place, rows, slabs, counts, *refs):
    blocks, refs = refs[:count], refs[count:]
    inv_own, inv_par, so_far, t_own, t_par, out, held, turned, kept, tiles, acc, rounded = refs[:12]
    applied, found_rows, found_count, unit_sems, sum_sems, tile_sems, out_sems = refs[12:]
    units = fetches(plan, place, blocks, inv_own, inv_par, held, turned, unit_sems)
    sums = [pltpu.make_async_copy(so_far.at[s], kept.at[s], sum_sems.at[s]) for s in range(HERE)]

    def tile_copies(s, l, slot):
        upper, lower = pl.ds(0, ROWS_HERE), pl.ds(ROWS_HERE, ROWS_HERE)
        return (
            pltpu.make_async_copy(t_own.at[s, l], tiles.at[s, slot, upper], tile_sems.at[s]),
            pltpu.make_async_copy(t_par.at[s, l], tiles.at[s, slot, lower], tile_sems.at[s]),
        )

    for s in range(HERE):
        for n, unit in enumerate(plan):
            if unit[0] == s:
                for copy in units[n]:
                    copy.start()
        sums[s].start()

        def look(l, found, s=s):
            hit = slabs[s, l] == place[2]

            @pl.when(hit)
            def _():
                found_rows[s, found] = rows[s, l]
                for copy in tile_copies(s, l, found):
                    copy.start()

            return found + hit.astype(jnp.int32)

        found_count[s] = lax.fori_loop(0, counts[s], look, jnp.int32(0))
    acc[...] = jnp.zeros_like(acc)
    for s in range(HERE):
        total = added(s, plan, units, held, turned)
        sums[s].wait()
        applied[...] = (total + kept[s]).astype(jnp.bfloat16)
        found = found_count[s]

        def landed(slot, carry, s=s):
            for copy in tile_copies(s, 0, slot):
                copy.wait()
            return carry

        lax.fori_loop(0, found, landed, 0)

        def step(b, carry, s=s, found=found):
            left = jnp.concatenate([tiles[s, b * BATCH + j].T for j in range(BATCH)], axis=0)
            term = jnp.dot(left, applied[...], preferred_element_type=jnp.float32)
            for j in range(BATCH):

                @pl.when(b * BATCH + j < found)
                def _():
                    acc[found_rows[s, b * BATCH + j]] += term[j * TILE : (j + 1) * TILE]

            return carry

        lax.fori_loop(0, (found + BATCH - 1) // BATCH, step, 0)
    writes = []
    for part in range(4):
        span = pl.ds(part * (NTILE // 4), NTILE // 4)
        rounded[span] = acc[span].astype(jnp.bfloat16)
        write = pltpu.make_async_copy(rounded.at[span], out.at[span], out_sems.at[part])
        write.start()
        writes.append(write)
    for write in writes:
        write.wait()


def couple(place, rows, slabs, counts, inv_own, inv_par, groups, so_far, t_own, t_par):
    operands, plan = layout(groups)
    units = len(plan)
    return pl.pallas_call(
        functools.partial(couple_body, plan, len(operands)),
        out_shape=jax.ShapeDtypeStruct((NTILE, TILE, SLAB_W), jnp.bfloat16),
        in_specs=[SCALAR] * 4 + [ANY] * (len(operands) + 5),
        out_specs=ANY,
        scratch_shapes=[
            pltpu.VMEM((units, CHIP_ROWS, SLAB_W), jnp.bfloat16),
            pltpu.VMEM((units, CHIP_ROWS, CHIP_ROWS), jnp.bfloat16),
            pltpu.VMEM((HERE, CHIP_ROWS, SLAB_W), jnp.float32),
            pltpu.VMEM((HERE, LIST, CHIP_ROWS, TILE), jnp.bfloat16),
            pltpu.VMEM((NTILE, TILE, SLAB_W), jnp.float32),
            pltpu.VMEM((NTILE, TILE, SLAB_W), jnp.bfloat16),
            pltpu.VMEM((CHIP_ROWS, SLAB_W), jnp.bfloat16),
            pltpu.SMEM((HERE, LIST), jnp.int32),
            pltpu.SMEM((HERE,), jnp.int32),
            pltpu.SemaphoreType.DMA((units,)),
            pltpu.SemaphoreType.DMA((HERE,)),
            pltpu.SemaphoreType.DMA((HERE,)),
            pltpu.SemaphoreType.DMA((4,)),
        ],
        cost_estimate=pl.CostEstimate(flops=3 << 30, bytes_accessed=12 << 20, transcendentals=0),
        name="couple",
    )(
        place,
        rows,
        slabs,
        counts,
        *operands,
        inv_own,
        inv_par,
        so_far,
        t_own,
        t_par,
    )


def to_all(array, axes, size):
    return lax.all_to_all(
        jnp.broadcast_to(array[None], (size, *array.shape)), axes, 0, 0, tiled=True
    )


def earlier_term(earlier_panels, used_panels, xh, z, c):
    chosen = earlier_panels[used_panels]
    top = to_all(chosen, ("y", "xl"), 8)[0]
    prev = moved(top, dz=1)
    after = moved(top, dz=-1)
    opposite = moved(top, dz=2)
    line = jnp.stack([top, after, opposite, prev])
    plane = jnp.concatenate([line, moved(line, dx=2)], axis=0)
    both = jnp.concatenate([plane, moved(plane, dc=1)], axis=0)
    intr = jnp.arange(16, dtype=jnp.int32)
    far = lax.rem(intr // 8 + xh, 2)
    shift = lax.rem(intr // 2 % 4 + 4 - z, 4)
    other = lax.rem(intr % 2 + c, 2)
    ordered = both[other * 8 + far * 4 + shift]
    top_rows = ordered.transpose(1, 0, 2, 3).reshape(4, COLS, TILE)
    product = jnp.einsum("prt,pct->rc", chosen, top_rows, preferred_element_type=jnp.float32)
    return lax.optimization_barrier(product)


def on_device(
    inverse_panels,
    border_columns,
    border_tiles,
    tile_rows,
    tile_slabs,
    tile_count,
    base_slab,
    earlier_panels,
    used_panels,
):
    xh = lax.axis_index("xh")
    z = lax.axis_index("z")
    c = lax.axis_index("c")
    place = jnp.stack([xh, z, c]).astype(jnp.int32)

    low, high = border_columns[:, :, :SLAB_W], border_columns[:, :, SLAB_W:]
    got = moved(jnp.where(c == 0, high, low), dc=1)
    mine = jnp.where(
        c == 0, jnp.concatenate([low, got], axis=1), jnp.concatenate([got, high], axis=1)
    )
    inv_par = moved(inverse_panels, dc=1)
    t_par = moved(border_tiles, dc=1)

    a0, b0 = mine[:2], mine[2:]
    bx = moved(b0, dx=2)
    ap = moved(a0, dz=-1)
    am = moved(a0, dz=1)
    xa0 = moved(a0, dx=2)
    bb = jnp.concatenate([b0, bx], axis=0)
    bp = moved(bb, dz=-1)
    bm = moved(bb, dz=1)
    a2 = moved(am, dz=1)
    xa1 = moved(jnp.concatenate([am, ap], axis=0), dx=2)
    xa2 = moved(a2, dx=2)
    b2a = moved(bp[:3], dz=-1)
    b2b = moved(bm[3:], dz=1)

    near, far = 0, 1
    so_far = stage(
        place,
        inverse_panels,
        inv_par,
        [
            [
                (a0, g, (near, 0)),
                (am, g, (near, 3)),
                (ap, g, (near, 1)),
                (a2, g, (near, 2)),
                (xa0, g, (far, 0)),
            ]
            for g in range(2)
        ]
        + [
            [
                (bb, g, (near, 0)),
                (bb, 2 + g, (far, 0)),
            ]
            for g in range(2)
        ],
    )
    so_far = stage(
        place,
        inverse_panels,
        inv_par,
        [[]] * 2 + [[(bp, g, (near, 1)), (bp, 2 + g, (far, 1))] for g in range(2)],
        so_far,
    )
    so_far = stage(
        place,
        inverse_panels,
        inv_par,
        [[(xa1, g, (far, 3)), (xa1, 2 + g, (far, 1))] for g in range(2)]
        + [[(bm, g, (near, 3)), (bm, 2 + g, (far, 3))] for g in range(2)],
        so_far,
    )
    part = couple(
        place,
        tile_rows,
        tile_slabs,
        tile_count,
        inverse_panels,
        inv_par,
        [
            [(xa2, 0, (far, 2))],
            [(xa2, 1, (far, 2))],
            [(b2a, 0, (near, 2)), (b2a, 2, (far, 2))],
            [(b2a, 1, (near, 2)), (b2b, 0, (far, 2))],
        ],
        so_far,
        border_tiles,
        t_par,
    )
    earlier = earlier_term(earlier_panels, used_panels, xh, z, c)
    spread = lax.all_to_all(part.reshape(4096, SLAB_W), CHIPS, 0, 0, tiled=True)
    total = spread.reshape(64, 2, 32, SLAB_W).astype(jnp.float32).sum(axis=0)
    held = jnp.where(c == 0, total[0], total[1])
    got = moved(jnp.where(c == 0, total[1], total[0]), dc=1)
    coupling = jnp.concatenate(
        [jnp.where(c == 0, held, got), jnp.where(c == 0, got, held)], axis=1
    )
    return base_slab - coupling - earlier


def solution(mesh):
    split = jax.sharding.Mesh(mesh.devices.reshape(4, 2, 2, 4, 2), AXES)
    scen, intr = ("y", "xl"), ("xh", "z", "c")
    return jax.shard_map(
        on_device,
        mesh=split,
        in_specs=(
            P(scen, intr, None),
            P(scen, intr, None),
            P(scen, None, intr, None),
            P(scen, None),
            P(scen, None),
            P(scen),
            P(AXES, None),
            P(None, AXES, None),
            P(),
        ),
        out_specs=P(AXES, None),
        check_vma=False,
    )
```
